128 devices in a mesh: section: 4 (over y_hi, core), frame: 32 (over y_lo, x, z).
Axes of the slice: x: 4, y: 4 (y_hi: 2, y_lo: 2; y = y_hi * 2 + y_lo), z: 4, core: 2. Of those that a mesh axis runs over, the one named last changes fastest.
Arguments:
- newcomer_groups: bfloat16 [1, 8192, 1536], P(None, 'frame'), may hold values from -6 to 6
- pending_inputs: bfloat16 [4, 8192, 1536], P('section', 'frame'), may hold values from -6 to 6
- speaker_clip_ids: int32 [5, 8192], P(None, 'frame'), may hold values from 0 to 63, never falling along the last dimension, each value on 1 to 256 neighbouring positions
- selfattend_scaling: float32 [4, 1536], P('section'), may hold values from 0.1 to 1.9
- triple_projection_matrix: bfloat16 [4, 1536, 4608], P('section', 'frame'), may hold values from -1 to 1
- selfattend_final_matrix: bfloat16 [4, 1536, 1536], P('section', 'frame'), may hold values from -0.15625 to 0.15625
- depthwise_scaling: float32 [4, 1536], P('section'), may hold values from 0.1 to 1.9
- sigmoid_expand_matrix: bfloat16 [4, 1536, 3072], P('section', 'frame'), may hold values from -0.15625 to 0.15625
- filter_taps: float32 [4, 31, 1536], P('section'), may hold values from -1 to 1
- combine_channel_matrix: bfloat16 [4, 1536, 1536], P('section', 'frame'), may hold values from -0.15625 to 0.15625
Outputs:
- section_out: bfloat16 [2, 4, 8192, 1536], P(None, 'section', 'frame')
The draws below stay inside these ranges and needn't reach their ends.
Inputs may be any that keep to these rules, and one draw needn't show every extreme that they name: `speaker_clip_ids`: in every row the ids never fall along frames; every utterance has 1 to 256 frames, and one utterance of each row has exactly 256.
All inputs are finite; a program needn't handle non-finite values.
Results may differ from the reference program's by a relative error of at most 0.008.
Values may be sent and summed in bfloat16 or wider, within the bound.
A program may use at most 192 MiB of HBM per device.

```python
import math
import jax
import jax.numpy as jnp
import numpy as np
from jax import lax

HIDDEN_FEATURE = 1536
HEADS = 24
HEAD_DIM = 64
KERNEL = 31
TOK_DEV = 256
TICKS = 2
HANDOFF_PARTS = 4
GROUP_SAMPLES = 8192
MB = 5
SEGS = 64
N_FRAME = 32


def draw_triple_projection_matrix(key, part):
    scale = HIDDEN_FEATURE ** (-0.5)
    base = jax.random.normal(key, (HANDOFF_PARTS, HIDDEN_FEATURE, 3 * HIDDEN_FEATURE), jnp.float32)
    base = jnp.clip(base, -6.0, 6.0) * scale
    return base.astype(jnp.bfloat16)


def steps_of(stream_key, extent, shards, smallest, top_value):
    def one(position, blocks):
        heights = jax.random.uniform(jax.random.fold_in(jax.random.fold_in(stream_key, 6), position), (blocks,), jnp.float32, smallest / len(shards), top_value / len(shards))
        return jnp.repeat(jnp.exp(heights), extent[position] // blocks).reshape((-1,) + (1,) * (len(extent) - position - 1))

    factor_of = one(*shards[0])
    for cut in shards[1:]:
        factor_of = factor_of * one(*cut)
    return factor_of


def profile(amount, total, bound, lean):
    portions = [(1 << 20) // math.isqrt(grade ** lean) + 1 for grade in range(2, amount + 1)]
    spare, given = total - bound - (amount - 1), [1] * (amount - 1)
    while spare > 0:
        free = [i for i in range(amount - 1) if given[i] < bound]
        mass, remaining = sum([portions[i] for i in free]), spare
        for i in free:
            extra = min(bound - given[i], max(1, remaining * portions[i] // mass), spare)
            given[i] = given[i] + extra
            spare = spare - extra
    return np.array([bound] + given)


def uneven(own_key, count, total, reach, slope):
    if count == 2:
        one = jax.random.randint(own_key, (), max(1, total - reach), min(reach, total - 1) + 1)
        return jnp.stack([one, total - one])
    sizes = jnp.asarray(profile(count, total, reach, slope), jnp.int32)
    couples = (count - 1) // 2
    donor, sink = sizes[1:1 + 2 * couples:2], sizes[2:2 + 2 * couples:2]
    slack = jnp.minimum(donor - 1, reach - sink)
    passed = jax.random.randint(jax.random.fold_in(own_key, 1), (couples,), 0, 1 << 20) % (slack + 1)
    sizes = sizes.at[1:1 + 2 * couples:2].set(donor - passed).at[2:2 + 2 * couples:2].set(sink + passed)
    return sizes[jax.random.permutation(jax.random.fold_in(own_key, 2), count)]


def bell_draw(key, shape, scale, limit, shards=(), kind=jnp.bfloat16):
    values = jax.random.normal(key, shape, jnp.float32) * scale
    if len(shards) > 0:
        values = steps_of(key, shape, shards, -0.22, 0.18) * values
    return jnp.clip(values, min=-limit, max=limit).astype(kind)


def setup_inputs(seed: int = 0) -> dict:
    streams_of = jax.random.split(jax.random.key(seed), 11)
    newcomer_groups = bell_draw(streams_of[0], (TICKS - 1, GROUP_SAMPLES, HIDDEN_FEATURE), 1.0, 6.0, ((1, 32),))
    pending_inputs = bell_draw(streams_of[1], (HANDOFF_PARTS, GROUP_SAMPLES, HIDDEN_FEATURE), 1.0, 6.0, ((0, 4), (1, 32)))
    speaker_clip_ids = jax.vmap(lambda own: jnp.searchsorted(jnp.cumsum(uneven(own, SEGS, GROUP_SAMPLES, TOK_DEV, 0)), jnp.arange(GROUP_SAMPLES), side="right"))(jax.random.split(streams_of[2], MB)).reshape((MB, GROUP_SAMPLES)).astype(jnp.int32)
    selfattend_scaling = jnp.clip(1.0 + 0.18 * jax.random.normal(streams_of[3], (HANDOFF_PARTS, HIDDEN_FEATURE), jnp.float32), 0.1, 1.9)
    triple_projection_matrix = draw_triple_projection_matrix(jax.random.fold_in(streams_of[10], 71), 0)
    selfattend_final_matrix = bell_draw(streams_of[5], (HANDOFF_PARTS, HIDDEN_FEATURE, HIDDEN_FEATURE), HIDDEN_FEATURE ** -0.5, 0.15625, ((0, 4), (1, 32)))
    depthwise_scaling = jnp.clip(1.0 + 0.18 * jax.random.normal(streams_of[6], (HANDOFF_PARTS, HIDDEN_FEATURE), jnp.float32), 0.1, 1.9)
    sigmoid_expand_matrix = bell_draw(streams_of[7], (HANDOFF_PARTS, HIDDEN_FEATURE, 2 * HIDDEN_FEATURE), HIDDEN_FEATURE ** -0.5, 0.15625, ((0, 4), (1, 32)))
    filter_taps = bell_draw(streams_of[8], (HANDOFF_PARTS, KERNEL, HIDDEN_FEATURE), KERNEL ** -0.5, 1.0, ((0, 4),), jnp.float32)
    combine_channel_matrix = bell_draw(streams_of[9], (HANDOFF_PARTS, HIDDEN_FEATURE, HIDDEN_FEATURE), HIDDEN_FEATURE ** -0.5, 0.15625, ((0, 4), (1, 32)))
    return dict(newcomer_groups=newcomer_groups, pending_inputs=pending_inputs, speaker_clip_ids=speaker_clip_ids, selfattend_scaling=selfattend_scaling, triple_projection_matrix=triple_projection_matrix, selfattend_final_matrix=selfattend_final_matrix, depthwise_scaling=depthwise_scaling, sigmoid_expand_matrix=sigmoid_expand_matrix, filter_taps=filter_taps, combine_channel_matrix=combine_channel_matrix)


EPS = 1e-05

def layer_norm(sample_lines, gain):
    mean = lax.optimization_barrier(jnp.mean(sample_lines, axis=-1, keepdims=True))
    centred = sample_lines - mean
    spread = lax.optimization_barrier(jnp.mean(centred * centred, axis=-1, keepdims=True))
    return centred * lax.rsqrt(spread + EPS) * gain

def attend_block(query, wide_keys, wide_values, seg_wide, seg_own):
    sample_lines = query.shape[0]
    shaped_q = query.astype(jnp.float32).reshape(sample_lines, HEADS, HEAD_DIM)
    shaped_k = wide_keys.astype(jnp.float32).reshape(wide_keys.shape[0], HEADS, HEAD_DIM)
    shaped_v = wide_values.astype(jnp.float32).reshape(wide_values.shape[0], HEADS, HEAD_DIM)
    scores = jnp.einsum('qhd,khd->hqk', shaped_q, shaped_k)
    allowed = (seg_own[:, None] == seg_wide[None, :])[None]
    scores = jnp.where(allowed, scores, -1e+30)
    top = lax.optimization_barrier(jnp.max(scores, axis=-1, keepdims=True))
    expd = jnp.exp(scores - top)
    probs = (expd / lax.optimization_barrier(jnp.sum(expd, axis=-1, keepdims=True))).astype(jnp.bfloat16)
    context = jnp.einsum('hqk,khd->qhd', probs.astype(jnp.float32), shaped_v)
    return context.astype(jnp.bfloat16).reshape(sample_lines, HIDDEN_FEATURE)

def depthwise(wide_glu, seg_conv, seg_own, taps):
    sample_lines = seg_own.shape[0]
    total = jnp.zeros((sample_lines, wide_glu.shape[1]), jnp.float32)
    for tap in range(taps.shape[0]):
        same = (seg_conv[tap:tap + sample_lines] == seg_own)[:, None]
        total = total + jnp.where(same, wide_glu[tap:tap + sample_lines].astype(jnp.float32) * taps[tap], 0.0)
    return total

def block(present_activity, seg, gain_a, wq, wo, gain_c, wg, taps, wm):
    resid = present_activity.astype(jnp.float32)
    normed = layer_norm(resid, gain_a).astype(jnp.bfloat16)
    projected = jnp.dot(normed, wq, preferred_element_type=jnp.float32)
    query = (projected[:, :HIDDEN_FEATURE] * HEAD_DIM ** (-0.5)).astype(jnp.bfloat16)
    keys = projected[:, HIDDEN_FEATURE:2 * HIDDEN_FEATURE].astype(jnp.bfloat16)
    values = projected[:, 2 * HIDDEN_FEATURE:].astype(jnp.bfloat16)
    empty = jnp.zeros((TOK_DEV, HIDDEN_FEATURE), jnp.bfloat16)
    keys_pad = jnp.concatenate([empty, keys, empty], axis=0)
    values_pad = jnp.concatenate([empty, values, empty], axis=0)
    outside = jnp.full((TOK_DEV,), -1, jnp.int32)
    seg_pad = jnp.concatenate([outside, seg.astype(jnp.int32), outside], axis=0)

    def one_block(index):
        start = (index * TOK_DEV).astype(jnp.int32)
        block_q = lax.dynamic_slice_in_dim(query, start, TOK_DEV, 0)
        block_k = lax.dynamic_slice_in_dim(keys_pad, start, 3 * TOK_DEV, 0)
        block_v = lax.dynamic_slice_in_dim(values_pad, start, 3 * TOK_DEV, 0)
        block_s = lax.dynamic_slice_in_dim(seg_pad, start, 3 * TOK_DEV, 0)
        own_s = lax.dynamic_slice_in_dim(seg.astype(jnp.int32), start, TOK_DEV, 0)
        return attend_block(block_q, block_k, block_v, block_s, own_s)
    context = lax.map(one_block, jnp.arange(N_FRAME, dtype=jnp.int32)).reshape(GROUP_SAMPLES, HIDDEN_FEATURE)
    resid = resid + jnp.dot(context, wo, preferred_element_type=jnp.float32)
    conv_in = layer_norm(resid, gain_c).astype(jnp.bfloat16)
    doubled = jnp.dot(conv_in, wg, preferred_element_type=jnp.float32)
    glu = (doubled[:, :HIDDEN_FEATURE] * jax.nn.sigmoid(doubled[:, HIDDEN_FEATURE:])).astype(jnp.bfloat16)
    half = KERNEL // 2
    rim = jnp.zeros((half, HIDDEN_FEATURE), jnp.bfloat16)
    glu_pad = jnp.concatenate([rim, glu, rim], axis=0)
    seg_rim = jnp.full((half,), -1, jnp.int32)
    seg_conv = jnp.concatenate([seg_rim, seg.astype(jnp.int32), seg_rim], axis=0)
    depth = depthwise(glu_pad, seg_conv, seg.astype(jnp.int32), taps)
    act = (depth * jax.nn.sigmoid(depth)).astype(jnp.bfloat16)
    resid = resid + jnp.dot(act, wm, preferred_element_type=jnp.float32)
    return resid.astype(jnp.bfloat16)

def reference(newcomer_groups, pending_inputs, speaker_clip_ids, selfattend_scaling, triple_projection_matrix, selfattend_final_matrix, depthwise_scaling, sigmoid_expand_matrix, filter_taps, combine_channel_matrix):
    present_activity = [pending_inputs[part_number] for part_number in range(HANDOFF_PARTS)]
    results = []
    for tick in range(TICKS):
        made = []
        for part_number in range(HANDOFF_PARTS):
            batch_index = HANDOFF_PARTS - 1 - part_number + tick
            made.append(block(present_activity[part_number], speaker_clip_ids[batch_index], selfattend_scaling[part_number], triple_projection_matrix[part_number], selfattend_final_matrix[part_number], depthwise_scaling[part_number], sigmoid_expand_matrix[part_number], filter_taps[part_number], combine_channel_matrix[part_number]))
        results.append(jnp.stack(made))
        if tick + 1 < TICKS:
            present_activity = [newcomer_groups[tick]] + made[:-1]
    return jnp.stack(results)
```

```python
import jax
import jax.numpy as jnp
from jax import lax
from jax.sharding import Mesh, PartitionSpec as P

HEADS = 24
KERNEL = 31


EPS = 1e-05
FRAME = ("yl", "x", "z")


def shift_ring(value, axis, steps):
    count = lax.axis_size(axis)
    return lax.ppermute(value, axis, [(i, (i + steps) % count) for i in range(count)])


def ring2(blocks, axis):
    return jnp.concatenate([blocks, shift_ring(blocks, axis, 1)], axis=0)


def ring4(blocks, axis):
    plus = shift_ring(blocks, axis, 1)
    minus = shift_ring(blocks, axis, -1)
    half = blocks.shape[-1] // 2
    opposite = jnp.concatenate(
        [shift_ring(plus[..., :half], axis, 1), shift_ring(minus[..., half:], axis, -1)], axis=-1
    )
    return jnp.concatenate([blocks, minus, opposite, plus], axis=0)


def gather_rows(local):
    half = local.shape[1] // 2
    first = ring4(ring4(ring2(local[None, :, :half], "yl"), "x"), "z")
    second = ring4(ring4(ring2(local[None, :, half:], "yl"), "z"), "x")
    rows = local.shape[0] * first.shape[0]
    return first.reshape(rows, half), second.reshape(rows, local.shape[1] - half)


def relative_columns(value, swap):
    lines, width = value.shape
    sizes = (lax.axis_size("yl"), lax.axis_size("x"), lax.axis_size("z"))
    shaped = value.reshape(lines, *sizes, width // (sizes[0] * sizes[1] * sizes[2]))
    for dim, name in ((1, "yl"), (2, "x"), (3, "z")):
        shaped = jnp.roll(shaped, -lax.axis_index(name), axis=dim)
    order = (0, 2, 3, 1, 4) if swap else (0, 3, 2, 1, 4)
    return shaped.transpose(order).reshape(lines, width)


def gathered_dot(value, weights):
    first, second = weights
    return jnp.concatenate(
        [
            jnp.dot(relative_columns(value, False), first, preferred_element_type=jnp.float32),
            jnp.dot(relative_columns(value, True), second, preferred_element_type=jnp.float32),
        ],
        axis=1,
    )


def extended(block, sides, width):
    for axis, dim in sides:
        count = lax.axis_size(axis)
        forward = [(i, i + 1) for i in range(count - 1)]
        backward = [(target, source) for source, target in forward]
        low = lax.ppermute(
            lax.slice_in_dim(block, block.shape[dim] - width, None, axis=dim), axis, forward
        )
        high = lax.ppermute(lax.slice_in_dim(block, 0, width, axis=dim), axis, backward)
        block = jnp.concatenate([low, block, high], axis=dim)
    return block


def shifted(value, axis, steps):
    count = lax.axis_size(axis)
    leading, last = (max(0, -steps), min(count, count - steps))
    return lax.ppermute(value, axis, [(source, source + steps) for source in range(leading, last)])


def layer_norm(sample_lines, gain):
    mean = jnp.mean(sample_lines, axis=-1, keepdims=True)
    centred = sample_lines - mean
    spread = jnp.mean(centred * centred, axis=-1, keepdims=True)
    return centred * lax.rsqrt(spread + EPS) * gain


def attend(query, wide_keys, wide_values, seg_wide, seg_own):
    sample_lines, feature_count = query.shape
    head_dim = feature_count // HEADS
    shaped_q = query.reshape(sample_lines, HEADS, head_dim)
    shaped_k = wide_keys.reshape(wide_keys.shape[0], HEADS, head_dim)
    shaped_v = wide_values.reshape(wide_values.shape[0], HEADS, head_dim)
    scores = jnp.einsum("qhd,khd->hqk", shaped_q, shaped_k, preferred_element_type=jnp.float32)
    allowed = (seg_own[:, None] == seg_wide[None, :])[None]
    scores = jnp.where(allowed, scores, -1e30)
    top = jnp.max(scores, axis=-1, keepdims=True)
    expd = jnp.exp(scores - top)
    probs = (expd / jnp.sum(expd, axis=-1, keepdims=True)).astype(jnp.bfloat16)
    context = jnp.einsum("hqk,khd->qhd", probs, shaped_v, preferred_element_type=jnp.float32)
    return context.astype(jnp.bfloat16).reshape(sample_lines, feature_count)


def depthwise(wide_glu, seg_conv, seg_own, taps):
    sample_lines = seg_own.shape[0]
    total = jnp.zeros((sample_lines, wide_glu.shape[1]), jnp.float32)
    for tap in range(taps.shape[0]):
        same = (seg_conv[tap : tap + sample_lines] == seg_own)[:, None]
        total = total + jnp.where(
            same, wide_glu[tap : tap + sample_lines].astype(jnp.float32) * taps[tap], 0.0
        )
    return total


def on_device(
    newcomer_groups,
    pending_inputs,
    speaker_clip_ids,
    selfattend_scaling,
    triple_projection_matrix,
    selfattend_final_matrix,
    depthwise_scaling,
    sigmoid_expand_matrix,
    filter_taps,
    combine_channel_matrix,
):
    sample_lines = pending_inputs.shape[1]
    feature_count = pending_inputs.shape[2]
    half = KERNEL // 2
    sections = lax.axis_size("section")
    section = lax.axis_index("section")
    ticks = newcomer_groups.shape[0] + 1
    seg_all = extended(speaker_clip_ids + 1, ((FRAME, 1),), sample_lines)
    full_qkv, full_out, full_glu, full_mix = (
        gather_rows(triple_projection_matrix[0]),
        gather_rows(selfattend_final_matrix[0]),
        gather_rows(sigmoid_expand_matrix[0]),
        gather_rows(combine_channel_matrix[0]),
    )
    present_activity = pending_inputs[0]
    made_all = []
    for tick in range(ticks):
        batch_index = sections - 1 - section + tick
        seg_wide = lax.dynamic_index_in_dim(seg_all, batch_index, 0, keepdims=False)
        seg_own = seg_wide[sample_lines : 2 * sample_lines]
        resid = present_activity.astype(jnp.float32)
        normed = layer_norm(resid, selfattend_scaling[0]).astype(jnp.bfloat16)
        projected = gathered_dot(normed, full_qkv)
        query = (projected[:, :feature_count] * (feature_count // HEADS) ** (-0.5)).astype(
            jnp.bfloat16
        )
        keys = projected[:, feature_count : 2 * feature_count].astype(jnp.bfloat16)
        values = projected[:, 2 * feature_count :].astype(jnp.bfloat16)
        wide_keys, wide_values = (
            extended(keys, ((FRAME, 0),), sample_lines),
            extended(values, ((FRAME, 0),), sample_lines),
        )
        context = attend(query, wide_keys, wide_values, seg_wide, seg_own)
        resid = resid + gathered_dot(context, full_out)
        conv_in = layer_norm(resid, depthwise_scaling[0]).astype(jnp.bfloat16)
        doubled = gathered_dot(conv_in, full_glu)
        glu = (doubled[:, :feature_count] * jax.nn.sigmoid(doubled[:, feature_count:])).astype(
            jnp.bfloat16
        )
        wide_glu = extended(glu, ((FRAME, 0),), half)
        depth = depthwise(
            wide_glu,
            seg_wide[sample_lines - half : 2 * sample_lines + half],
            seg_own,
            filter_taps[0],
        )
        act = (depth * jax.nn.sigmoid(depth)).astype(jnp.bfloat16)
        resid = resid + gathered_dot(act, full_mix)
        made = resid.astype(jnp.bfloat16)
        made_all.append(made)
        if tick + 1 < ticks:
            arrived = shifted(made, "section", 1)
            present_activity = jnp.where(section == 0, newcomer_groups[tick], arrived)
    return jnp.stack(made_all)[:, None]


def solution(mesh):
    sections = mesh.shape["section"]
    frames = mesh.shape["frame"]
    mesh = Mesh(mesh.devices.reshape(sections, 2, 4, frames // 8), ("section",) + FRAME)
    in_specs = (
        P(None, FRAME, None),
        P("section", FRAME, None),
        P(None, FRAME),
        P("section", None),
        P("section", FRAME, None),
        P("section", FRAME, None),
        P("section", None),
        P("section", FRAME, None),
        P("section", None, None),
        P("section", FRAME, None),
    )
    out_specs = P(None, "section", FRAME, None)
    return jax.shard_map(
        on_device, mesh=mesh, in_specs=in_specs, out_specs=out_specs, check_vma=False
    )
```

```python
import functools

import jax
import jax.numpy as jnp
from jax import lax
from jax.experimental import pallas as pl
from jax.experimental.pallas import tpu as pltpu
from jax.sharding import Mesh, PartitionSpec as P

HEADS = 24
KERNEL = 31


EPS = 1e-05
FRAME = ("yl", "x", "z")
MESH_AXES = ("section",) + FRAME


def gather_kernel(count, *refs):
    local, gathered = refs[:count], refs[count : 2 * count]
    own_sem, send_sem, recv_sem = refs[2 * count :]
    sizes = {name: lax.axis_size(name) for name in FRAME}
    here = {name: lax.axis_index(name) for name in MESH_AXES}

    def position(coords):
        return (coords["yl"] * sizes["x"] + coords["x"]) * sizes["z"] + coords["z"]

    def moved(coords, name, step):
        if step == 0:
            return coords
        other = dict(coords)
        other[name] = lax.rem(coords[name] + step + sizes[name], sizes[name])
        return other

    neighbours = [moved(here, "yl", 1)]
    for name in ("x", "z"):
        neighbours += [moved(here, name, 1), moved(here, name, -1)]
    barrier = pltpu.get_barrier_semaphore()
    for other in neighbours:
        pl.semaphore_signal(
            barrier, inc=1, device_id=tuple(other[a] for a in MESH_AXES),
            device_id_type=pl.DeviceIdType.MESH,
        )
    pl.semaphore_wait(barrier, len(neighbours))

    own_copies = []
    for w in range(count):
        copy = pltpu.make_async_copy(local[w], gathered[w].at[position(here)], own_sem.at[w])
        copy.start()
        own_copies.append(copy)

    counter = [0]

    def send(w, coords, cols, target):
        index = counter[0]
        counter[0] += 1
        if coords is here:
            source = local[w].at[:, cols]
        else:
            source = gathered[w].at[position(coords), :, cols]
        copy = pltpu.make_async_remote_copy(
            src_ref=source,
            dst_ref=gathered[w].at[position(coords), :, cols],
            send_sem=send_sem.at[index],
            recv_sem=recv_sem.at[index],
            device_id=tuple(target[a] for a in MESH_AXES),
            device_id_type=pl.DeviceIdType.MESH,
        )
        copy.start()
        return copy

    widths = [r.shape[-1] for r in local]
    orders = (("x", "z"), ("z", "x"))
    held = [[[here] for _ in orders] for _ in range(count)]

    def stripe_cols(w, s, part=None):
        half = widths[w] // 2
        lo, width = (0, half) if s == 0 else (half, widths[w] - half)
        if part is None:
            return pl.ds(lo, width)
        quarter = width // 2
        return pl.ds(lo, quarter) if part == 0 else pl.ds(lo + quarter, width - quarter)

    pending = []
    for w in range(count):
        for s in range(len(orders)):
            pending.append(send(w, here, stripe_cols(w, s), moved(here, "yl", 1)))
            held[w][s] = [here, moved(here, "yl", 1)]
    for copy in pending:
        copy.wait()
    for level in range(2):
        pending = []
        for w in range(count):
            for s, order in enumerate(orders):
                name = order[level]
                for coords in held[w][s]:
                    for step in (1, -1):
                        pending.append(send(w, coords, stripe_cols(w, s), moved(here, name, step)))
        for copy in pending:
            copy.wait()
        pending = []
        for w in range(count):
            for s, order in enumerate(orders):
                name = order[level]
                for coords in held[w][s]:
                    pending.append(
                        send(w, moved(coords, name, -1), stripe_cols(w, s, 0), moved(here, name, 1))
                    )
                    pending.append(
                        send(w, moved(coords, name, 1), stripe_cols(w, s, 1), moved(here, name, -1))
                    )
        for copy in pending:
            copy.wait()
        for w in range(count):
            for s, order in enumerate(orders):
                name = order[level]
                held[w][s] = [moved(c, name, step) for c in held[w][s] for step in (0, 1, 2, 3)]
    for copy in own_copies:
        copy.wait()


def gather_weights(blocks):
    count = len(blocks)
    frames = 1
    for name in FRAME:
        frames *= lax.axis_size(name)
    copies = count * 2 * (1 + 2 * (4 + 4 * 4))
    outs = pl.pallas_call(
        functools.partial(gather_kernel, count),
        out_shape=[jax.ShapeDtypeStruct((frames,) + b.shape, b.dtype) for b in blocks],
        in_specs=[pl.BlockSpec(memory_space=pl.ANY)] * count,
        out_specs=[pl.BlockSpec(memory_space=pl.ANY)] * count,
        scratch_shapes=[
            pltpu.SemaphoreType.DMA((count,)),
            pltpu.SemaphoreType.DMA((copies,)),
            pltpu.SemaphoreType.DMA((copies,)),
        ],
        compiler_params=pltpu.CompilerParams(collective_id=0, has_side_effects=True),
    )(*blocks)
    return [o.reshape(frames * o.shape[1], o.shape[2]) for o in outs]


def extended(block, sides, width):
    for axis, dim in sides:
        count = lax.axis_size(axis)
        forward = [(i, i + 1) for i in range(count - 1)]
        backward = [(target, source) for source, target in forward]
        low = lax.ppermute(
            lax.slice_in_dim(block, block.shape[dim] - width, None, axis=dim), axis, forward
        )
        high = lax.ppermute(lax.slice_in_dim(block, 0, width, axis=dim), axis, backward)
        block = jnp.concatenate([low, block, high], axis=dim)
    return block


def shifted(value, axis, steps):
    count = lax.axis_size(axis)
    leading, last = (max(0, -steps), min(count, count - steps))
    return lax.ppermute(value, axis, [(source, source + steps) for source in range(leading, last)])


def layer_norm(sample_lines, gain):
    mean = jnp.mean(sample_lines, axis=-1, keepdims=True)
    centred = sample_lines - mean
    spread = jnp.mean(centred * centred, axis=-1, keepdims=True)
    return centred * lax.rsqrt(spread + EPS) * gain


def attend(query, wide_keys, wide_values, seg_wide, seg_own):
    sample_lines, feature_count = query.shape
    head_dim = feature_count // HEADS
    shaped_q = query.reshape(sample_lines, HEADS, head_dim)
    shaped_k = wide_keys.reshape(wide_keys.shape[0], HEADS, head_dim)
    shaped_v = wide_values.reshape(wide_values.shape[0], HEADS, head_dim)
    scores = jnp.einsum("qhd,khd->hqk", shaped_q, shaped_k, preferred_element_type=jnp.float32)
    allowed = (seg_own[:, None] == seg_wide[None, :])[None]
    scores = jnp.where(allowed, scores, -1e30)
    top = jnp.max(scores, axis=-1, keepdims=True)
    expd = jnp.exp(scores - top)
    probs = (expd / jnp.sum(expd, axis=-1, keepdims=True)).astype(jnp.bfloat16)
    context = jnp.einsum("hqk,khd->qhd", probs, shaped_v, preferred_element_type=jnp.float32)
    return context.astype(jnp.bfloat16).reshape(sample_lines, feature_count)


def depthwise(wide_glu, seg_conv, seg_own, taps):
    sample_lines = seg_own.shape[0]
    total = jnp.zeros((sample_lines, wide_glu.shape[1]), jnp.float32)
    for tap in range(taps.shape[0]):
        same = (seg_conv[tap : tap + sample_lines] == seg_own)[:, None]
        total = total + jnp.where(
            same, wide_glu[tap : tap + sample_lines].astype(jnp.float32) * taps[tap], 0.0
        )
    return total


def on_device(
    newcomer_groups,
    pending_inputs,
    speaker_clip_ids,
    selfattend_scaling,
    triple_projection_matrix,
    selfattend_final_matrix,
    depthwise_scaling,
    sigmoid_expand_matrix,
    filter_taps,
    combine_channel_matrix,
):
    sample_lines = pending_inputs.shape[1]
    feature_count = pending_inputs.shape[2]
    half = KERNEL // 2
    sections = lax.axis_size("section")
    section = lax.axis_index("section")
    ticks = newcomer_groups.shape[0] + 1
    seg_all = extended(speaker_clip_ids + 1, ((FRAME, 1),), sample_lines)
    full_qkv, full_out, full_glu, full_mix = gather_weights(
        [
            triple_projection_matrix[0],
            selfattend_final_matrix[0],
            sigmoid_expand_matrix[0],
            combine_channel_matrix[0],
        ]
    )
    present_activity = pending_inputs[0]
    made_all = []
    for tick in range(ticks):
        batch_index = sections - 1 - section + tick
        seg_wide = lax.dynamic_index_in_dim(seg_all, batch_index, 0, keepdims=False)
        seg_own = seg_wide[sample_lines : 2 * sample_lines]
        resid = present_activity.astype(jnp.float32)
        normed = layer_norm(resid, selfattend_scaling[0]).astype(jnp.bfloat16)
        projected = jnp.dot(normed, full_qkv, preferred_element_type=jnp.float32)
        query = (projected[:, :feature_count] * (feature_count // HEADS) ** (-0.5)).astype(
            jnp.bfloat16
        )
        keys = projected[:, feature_count : 2 * feature_count].astype(jnp.bfloat16)
        values = projected[:, 2 * feature_count :].astype(jnp.bfloat16)
        wide_keys, wide_values = (
            extended(keys, ((FRAME, 0),), sample_lines),
            extended(values, ((FRAME, 0),), sample_lines),
        )
        context = attend(query, wide_keys, wide_values, seg_wide, seg_own)
        resid = resid + jnp.dot(context, full_out, preferred_element_type=jnp.float32)
        conv_in = layer_norm(resid, depthwise_scaling[0]).astype(jnp.bfloat16)
        doubled = jnp.dot(conv_in, full_glu, preferred_element_type=jnp.float32)
        glu = (doubled[:, :feature_count] * jax.nn.sigmoid(doubled[:, feature_count:])).astype(
            jnp.bfloat16
        )
        wide_glu = extended(glu, ((FRAME, 0),), half)
        depth = depthwise(
            wide_glu,
            seg_wide[sample_lines - half : 2 * sample_lines + half],
            seg_own,
            filter_taps[0],
        )
        act = (depth * jax.nn.sigmoid(depth)).astype(jnp.bfloat16)
        resid = resid + jnp.dot(act, full_mix, preferred_element_type=jnp.float32)
        made = resid.astype(jnp.bfloat16)
        made_all.append(made)
        if tick + 1 < ticks:
            arrived = shifted(made, "section", 1)
            present_activity = jnp.where(section == 0, newcomer_groups[tick], arrived)
    return jnp.stack(made_all)[:, None]


def solution(mesh):
    sections = mesh.shape["section"]
    frames = mesh.shape["frame"]
    mesh = Mesh(mesh.devices.reshape(sections, 2, 4, frames // 8), MESH_AXES)
    in_specs = (
        P(None, FRAME, None),
        P("section", FRAME, None),
        P(None, FRAME),
        P("section", None),
        P("section", FRAME, None),
        P("section", FRAME, None),
        P("section", None),
        P("section", FRAME, None),
        P("section", None, None),
        P("section", FRAME, None),
    )
    out_specs = P(None, "section", FRAME, None)
    return jax.shard_map(
        on_device, mesh=mesh, in_specs=in_specs, out_specs=out_specs, check_vma=False
    )
```

```python
import functools

import jax
import jax.numpy as jnp
from jax import lax
from jax.experimental import pallas as pl
from jax.experimental.pallas import tpu as pltpu
from jax.sharding import Mesh, PartitionSpec as P

HEADS = 24
KERNEL = 31


EPS = 1e-05
FRAME = ("yl", "x", "z")
MESH_AXES = ("section",) + FRAME


def gather_kernel(count, *refs):
    local, gathered = refs[:count], refs[count : 2 * count]
    own_sem, send_sem, recv_sem = refs[2 * count :]
    sizes = {name: lax.axis_size(name) for name in FRAME}
    here = {name: lax.axis_index(name) for name in MESH_AXES}

    def position(coords):
        return (coords["yl"] * sizes["x"] + coords["x"]) * sizes["z"] + coords["z"]

    def moved(coords, name, step):
        if step == 0:
            return coords
        other = dict(coords)
        other[name] = lax.rem(coords[name] + step + sizes[name], sizes[name])
        return other

    neighbours = [moved(here, "yl", 1)]
    for name in ("x", "z"):
        neighbours += [moved(here, name, 1), moved(here, name, -1)]
    barrier = pltpu.get_barrier_semaphore()
    for other in neighbours:
        pl.semaphore_signal(
            barrier, inc=1, device_id=tuple(other[a] for a in MESH_AXES),
            device_id_type=pl.DeviceIdType.MESH,
        )
    pl.semaphore_wait(barrier, len(neighbours))

    own_copies = []
    for w in range(count):
        copy = pltpu.make_async_copy(local[w], gathered[w].at[position(here)], own_sem.at[w])
        copy.start()
        own_copies.append(copy)

    counter = [0]

    def send(w, coords, cols, target):
        index = counter[0]
        counter[0] += 1
        if coords is here:
            source = local[w].at[:, cols]
        else:
            source = gathered[w].at[position(coords), :, cols]
        copy = pltpu.make_async_remote_copy(
            src_ref=source,
            dst_ref=gathered[w].at[position(coords), :, cols],
            send_sem=send_sem.at[index],
            recv_sem=recv_sem.at[index],
            device_id=tuple(target[a] for a in MESH_AXES),
            device_id_type=pl.DeviceIdType.MESH,
        )
        copy.start()
        return copy

    widths = [r.shape[-1] for r in local]
    orders = (("x", "z"), ("z", "x"))
    held = [[[here] for _ in orders] for _ in range(count)]

    def stripe_cols(w, s, part=None):
        half = widths[w] // 2
        lo, width = (0, half) if s == 0 else (half, widths[w] - half)
        if part is None:
            return pl.ds(lo, width)
        quarter = width // 2
        return pl.ds(lo, quarter) if part == 0 else pl.ds(lo + quarter, width - quarter)

    pending = []
    for w in range(count):
        for s in range(len(orders)):
            pending.append(send(w, here, stripe_cols(w, s), moved(here, "yl", 1)))
            held[w][s] = [here, moved(here, "yl", 1)]
    for copy in pending:
        copy.wait()
    for level in range(2):
        pending = []
        for w in range(count):
            for s, order in enumerate(orders):
                name = order[level]
                for coords in held[w][s]:
                    for step in (1, -1):
                        pending.append(send(w, coords, stripe_cols(w, s), moved(here, name, step)))
        for copy in pending:
            copy.wait()
        pending = []
        for w in range(count):
            for s, order in enumerate(orders):
                name = order[level]
                for coords in held[w][s]:
                    pending.append(
                        send(w, moved(coords, name, -1), stripe_cols(w, s, 0), moved(here, name, 1))
                    )
                    pending.append(
                        send(w, moved(coords, name, 1), stripe_cols(w, s, 1), moved(here, name, -1))
                    )
        for copy in pending:
            copy.wait()
        for w in range(count):
            for s, order in enumerate(orders):
                name = order[level]
                held[w][s] = [moved(c, name, step) for c in held[w][s] for step in (0, 1, 2, 3)]
    for copy in own_copies:
        copy.wait()


def gather_weights(blocks):
    count = len(blocks)
    frames = 1
    for name in FRAME:
        frames *= lax.axis_size(name)
    copies = count * 2 * (1 + 2 * (4 + 4 * 4))
    outs = pl.pallas_call(
        functools.partial(gather_kernel, count),
        out_shape=[jax.ShapeDtypeStruct((frames,) + b.shape, b.dtype) for b in blocks],
        in_specs=[pl.BlockSpec(memory_space=pl.ANY)] * count,
        out_specs=[pl.BlockSpec(memory_space=pl.ANY)] * count,
        scratch_shapes=[
            pltpu.SemaphoreType.DMA((count,)),
            pltpu.SemaphoreType.DMA((copies,)),
            pltpu.SemaphoreType.DMA((copies,)),
        ],
        compiler_params=pltpu.CompilerParams(collective_id=0, has_side_effects=True),
    )(*blocks)
    return [o.reshape(frames * o.shape[1], o.shape[2]) for o in outs]


def extended(block, sides, width):
    for axis, dim in sides:
        count = lax.axis_size(axis)
        forward = [(i, i + 1) for i in range(count - 1)]
        backward = [(target, source) for source, target in forward]
        low = lax.ppermute(
            lax.slice_in_dim(block, block.shape[dim] - width, None, axis=dim), axis, forward
        )
        high = lax.ppermute(lax.slice_in_dim(block, 0, width, axis=dim), axis, backward)
        block = jnp.concatenate([low, block, high], axis=dim)
    return block


def shifted(value, axis, steps):
    count = lax.axis_size(axis)
    leading, last = (max(0, -steps), min(count, count - steps))
    return lax.ppermute(value, axis, [(source, source + steps) for source in range(leading, last)])


def layer_norm(sample_lines, gain):
    mean = jnp.mean(sample_lines, axis=-1, keepdims=True)
    centred = sample_lines - mean
    spread = jnp.mean(centred * centred, axis=-1, keepdims=True)
    return centred * lax.rsqrt(spread + EPS) * gain


def attend(query, wide_keys, wide_values, seg_wide, seg_own):
    sample_lines, feature_count = query.shape
    head_dim = feature_count // HEADS
    shaped_q = query.reshape(sample_lines, HEADS, head_dim)
    shaped_k = wide_keys.reshape(wide_keys.shape[0], HEADS, head_dim)
    shaped_v = wide_values.reshape(wide_values.shape[0], HEADS, head_dim)
    scores = jnp.einsum("qhd,khd->hqk", shaped_q, shaped_k, preferred_element_type=jnp.float32)
    allowed = (seg_own[:, None] == seg_wide[None, :])[None]
    scores = jnp.where(allowed, scores, -1e30)
    top = jnp.max(scores, axis=-1, keepdims=True)
    expd = jnp.exp(scores - top)
    probs = (expd / jnp.sum(expd, axis=-1, keepdims=True)).astype(jnp.bfloat16)
    context = jnp.einsum("hqk,khd->qhd", probs, shaped_v, preferred_element_type=jnp.float32)
    return context.astype(jnp.bfloat16).reshape(sample_lines, feature_count)


def depthwise(wide_glu, seg_conv, seg_own, taps):
    sample_lines = seg_own.shape[0]
    total = jnp.zeros((sample_lines, wide_glu.shape[1]), jnp.float32)
    for tap in range(taps.shape[0]):
        same = (seg_conv[tap : tap + sample_lines] == seg_own)[:, None]
        total = total + jnp.where(
            same, wide_glu[tap : tap + sample_lines].astype(jnp.float32) * taps[tap], 0.0
        )
    return total


def on_device(
    newcomer_groups,
    pending_inputs,
    speaker_clip_ids,
    selfattend_scaling,
    triple_projection_matrix,
    selfattend_final_matrix,
    depthwise_scaling,
    sigmoid_expand_matrix,
    filter_taps,
    combine_channel_matrix,
):
    sample_lines = pending_inputs.shape[1]
    feature_count = pending_inputs.shape[2]
    half = KERNEL // 2
    sections = lax.axis_size("section")
    section = lax.axis_index("section")
    ticks = newcomer_groups.shape[0] + 1
    seg_all = extended(speaker_clip_ids + 1, ((FRAME, 1),), sample_lines)
    full_mix = lax.all_gather(combine_channel_matrix[0], FRAME, axis=0, tiled=True)
    full_qkv, full_out, full_glu = gather_weights(
        [triple_projection_matrix[0], selfattend_final_matrix[0], sigmoid_expand_matrix[0]]
    )
    present_activity = pending_inputs[0]
    made_all = []
    for tick in range(ticks):
        batch_index = sections - 1 - section + tick
        seg_wide = lax.dynamic_index_in_dim(seg_all, batch_index, 0, keepdims=False)
        seg_own = seg_wide[sample_lines : 2 * sample_lines]
        resid = present_activity.astype(jnp.float32)
        normed = layer_norm(resid, selfattend_scaling[0]).astype(jnp.bfloat16)
        projected = jnp.dot(normed, full_qkv, preferred_element_type=jnp.float32)
        query = (projected[:, :feature_count] * (feature_count // HEADS) ** (-0.5)).astype(
            jnp.bfloat16
        )
        keys = projected[:, feature_count : 2 * feature_count].astype(jnp.bfloat16)
        values = projected[:, 2 * feature_count :].astype(jnp.bfloat16)
        wide_pairs = extended(jnp.concatenate([keys, values], axis=1), ((FRAME, 0),), sample_lines)
        wide_keys, wide_values = wide_pairs[:, :feature_count], wide_pairs[:, feature_count:]
        context = attend(query, wide_keys, wide_values, seg_wide, seg_own)
        resid = resid + jnp.dot(context, full_out, preferred_element_type=jnp.float32)
        conv_in = layer_norm(resid, depthwise_scaling[0]).astype(jnp.bfloat16)
        doubled = jnp.dot(conv_in, full_glu, preferred_element_type=jnp.float32)
        glu = (doubled[:, :feature_count] * jax.nn.sigmoid(doubled[:, feature_count:])).astype(
            jnp.bfloat16
        )
        wide_glu = extended(glu, ((FRAME, 0),), half)
        depth = depthwise(
            wide_glu,
            seg_wide[sample_lines - half : 2 * sample_lines + half],
            seg_own,
            filter_taps[0],
        )
        act = (depth * jax.nn.sigmoid(depth)).astype(jnp.bfloat16)
        resid = resid + jnp.dot(act, full_mix, preferred_element_type=jnp.float32)
        made = resid.astype(jnp.bfloat16)
        made_all.append(made)
        if tick + 1 < ticks:
            arrived = shifted(made, "section", 1)
            present_activity = jnp.where(section == 0, newcomer_groups[tick], arrived)
    return jnp.stack(made_all)[:, None]


def solution(mesh):
    sections = mesh.shape["section"]
    frames = mesh.shape["frame"]
    mesh = Mesh(mesh.devices.reshape(sections, 2, 4, frames // 8), MESH_AXES)
    in_specs = (
        P(None, FRAME, None),
        P("section", FRAME, None),
        P(None, FRAME),
        P("section", None),
        P("section", FRAME, None),
        P("section", FRAME, None),
        P("section", None),
        P("section", FRAME, None),
        P("section", None, None),
        P("section", FRAME, None),
    )
    out_specs = P(None, "section", FRAME, None)
    return jax.shard_map(
        on_device, mesh=mesh, in_specs=in_specs, out_specs=out_specs, check_vma=False
    )
```

```python
import functools

import jax
import jax.numpy as jnp
from jax import lax
from jax.experimental import pallas as pl
from jax.experimental.pallas import tpu as pltpu
from jax.sharding import Mesh, PartitionSpec as P

HEADS = 24
KERNEL = 31


EPS = 1e-05
FRAME = ("yl", "x", "z")
MESH_AXES = ("section",) + FRAME


def gather_kernel(count, *refs):
    local, gathered = refs[:count], refs[count : 2 * count]
    own_sem, send_sem, recv_sem = refs[2 * count :]
    sizes = {name: lax.axis_size(name) for name in FRAME}
    here = {name: lax.axis_index(name) for name in MESH_AXES}

    def position(coords):
        return (coords["yl"] * sizes["x"] + coords["x"]) * sizes["z"] + coords["z"]

    def moved(coords, name, step):
        if step == 0:
            return coords
        other = dict(coords)
        other[name] = lax.rem(coords[name] + step + sizes[name], sizes[name])
        return other

    neighbours = [moved(here, "yl", 1)]
    for name in ("x", "z"):
        neighbours += [moved(here, name, 1), moved(here, name, -1)]
    barrier = pltpu.get_barrier_semaphore()
    for other in neighbours:
        pl.semaphore_signal(
            barrier, inc=1, device_id=tuple(other[a] for a in MESH_AXES),
            device_id_type=pl.DeviceIdType.MESH,
        )
    pl.semaphore_wait(barrier, len(neighbours))

    own_copies = []
    for w in range(count):
        copy = pltpu.make_async_copy(local[w], gathered[w].at[position(here)], own_sem.at[w])
        copy.start()
        own_copies.append(copy)

    counter = [0]

    def send(w, coords, cols, target):
        index = counter[0]
        counter[0] += 1
        if coords is here:
            source = local[w].at[:, cols]
        else:
            source = gathered[w].at[position(coords), :, cols]
        copy = pltpu.make_async_remote_copy(
            src_ref=source,
            dst_ref=gathered[w].at[position(coords), :, cols],
            send_sem=send_sem.at[index],
            recv_sem=recv_sem.at[index],
            device_id=tuple(target[a] for a in MESH_AXES),
            device_id_type=pl.DeviceIdType.MESH,
        )
        copy.start()
        return copy

    widths = [r.shape[-1] for r in local]
    orders = (("x", "z"), ("z", "x"))
    held = [[[here] for _ in orders] for _ in range(count)]

    def stripe_cols(w, s, part=None):
        half = widths[w] // 2
        lo, width = (0, half) if s == 0 else (half, widths[w] - half)
        if part is None:
            return pl.ds(lo, width)
        quarter = width // 2
        return pl.ds(lo, quarter) if part == 0 else pl.ds(lo + quarter, width - quarter)

    pending = []
    for w in range(count):
        for s in range(len(orders)):
            pending.append(send(w, here, stripe_cols(w, s), moved(here, "yl", 1)))
            held[w][s] = [here, moved(here, "yl", 1)]
    for copy in pending:
        copy.wait()
    for level in range(2):
        pending = []
        for w in range(count):
            for s, order in enumerate(orders):
                name = order[level]
                for coords in held[w][s]:
                    for step in (1, -1):
                        pending.append(send(w, coords, stripe_cols(w, s), moved(here, name, step)))
        for copy in pending:
            copy.wait()
        pending = []
        for w in range(count):
            for s, order in enumerate(orders):
                name = order[level]
                for coords in held[w][s]:
                    pending.append(
                        send(w, moved(coords, name, -1), stripe_cols(w, s, 0), moved(here, name, 1))
                    )
                    pending.append(
                        send(w, moved(coords, name, 1), stripe_cols(w, s, 1), moved(here, name, -1))
                    )
        for copy in pending:
            copy.wait()
        for w in range(count):
            for s, order in enumerate(orders):
                name = order[level]
                held[w][s] = [moved(c, name, step) for c in held[w][s] for step in (0, 1, 2, 3)]
    for copy in own_copies:
        copy.wait()


def gather_weights(blocks):
    count = len(blocks)
    frames = 1
    for name in FRAME:
        frames *= lax.axis_size(name)
    copies = count * 2 * (1 + 2 * (4 + 4 * 4))
    outs = pl.pallas_call(
        functools.partial(gather_kernel, count),
        out_shape=[jax.ShapeDtypeStruct((frames,) + b.shape, b.dtype) for b in blocks],
        in_specs=[pl.BlockSpec(memory_space=pl.ANY)] * count,
        out_specs=[pl.BlockSpec(memory_space=pl.ANY)] * count,
        scratch_shapes=[
            pltpu.SemaphoreType.DMA((count,)),
            pltpu.SemaphoreType.DMA((copies,)),
            pltpu.SemaphoreType.DMA((copies,)),
        ],
        compiler_params=pltpu.CompilerParams(collective_id=0, has_side_effects=True),
    )(*blocks)
    return [o.reshape(frames * o.shape[1], o.shape[2]) for o in outs]


def extended(block, sides, width):
    for axis, dim in sides:
        count = lax.axis_size(axis)
        forward = [(i, i + 1) for i in range(count - 1)]
        backward = [(target, source) for source, target in forward]
        low = lax.ppermute(
            lax.slice_in_dim(block, block.shape[dim] - width, None, axis=dim), axis, forward
        )
        high = lax.ppermute(lax.slice_in_dim(block, 0, width, axis=dim), axis, backward)
        block = jnp.concatenate([low, block, high], axis=dim)
    return block


def shifted(value, axis, steps):
    count = lax.axis_size(axis)
    leading, last = (max(0, -steps), min(count, count - steps))
    return lax.ppermute(value, axis, [(source, source + steps) for source in range(leading, last)])


def layer_norm(sample_lines, gain):
    mean = jnp.mean(sample_lines, axis=-1, keepdims=True)
    centred = sample_lines - mean
    spread = jnp.mean(centred * centred, axis=-1, keepdims=True)
    return centred * lax.rsqrt(spread + EPS) * gain


def attend(query, wide_keys, wide_values, seg_wide, seg_own):
    sample_lines, feature_count = query.shape
    head_dim = feature_count // HEADS
    shaped_q = query.reshape(sample_lines, HEADS, head_dim)
    shaped_k = wide_keys.reshape(wide_keys.shape[0], HEADS, head_dim)
    shaped_v = wide_values.reshape(wide_values.shape[0], HEADS, head_dim)
    scores = jnp.einsum("qhd,khd->hqk", shaped_q, shaped_k, preferred_element_type=jnp.float32)
    allowed = (seg_own[:, None] == seg_wide[None, :])[None]
    scores = jnp.where(allowed, scores, -1e30)
    top = jnp.max(scores, axis=-1, keepdims=True)
    expd = jnp.exp(scores - top)
    probs = (expd / jnp.sum(expd, axis=-1, keepdims=True)).astype(jnp.bfloat16)
    context = jnp.einsum("hqk,khd->qhd", probs, shaped_v, preferred_element_type=jnp.float32)
    return context.astype(jnp.bfloat16).reshape(sample_lines, feature_count)


def depthwise(wide_glu, seg_conv, seg_own, taps):
    sample_lines = seg_own.shape[0]
    total = jnp.zeros((sample_lines, wide_glu.shape[1]), jnp.float32)
    for tap in range(taps.shape[0]):
        same = (seg_conv[tap : tap + sample_lines] == seg_own)[:, None]
        total = total + jnp.where(
            same, wide_glu[tap : tap + sample_lines].astype(jnp.float32) * taps[tap], 0.0
        )
    return total


def on_device(
    newcomer_groups,
    pending_inputs,
    speaker_clip_ids,
    selfattend_scaling,
    triple_projection_matrix,
    selfattend_final_matrix,
    depthwise_scaling,
    sigmoid_expand_matrix,
    filter_taps,
    combine_channel_matrix,
):
    sample_lines = pending_inputs.shape[1]
    feature_count = pending_inputs.shape[2]
    half = KERNEL // 2
    sections = lax.axis_size("section")
    section = lax.axis_index("section")
    ticks = newcomer_groups.shape[0] + 1
    seg_all = extended(speaker_clip_ids + 1, ((FRAME, 1),), sample_lines)
    full_qkv, full_out, full_glu, full_mix = gather_weights(
        [
            triple_projection_matrix[0],
            selfattend_final_matrix[0],
            sigmoid_expand_matrix[0],
            combine_channel_matrix[0],
        ]
    )
    present_activity = pending_inputs[0]
    made_all = []
    for tick in range(ticks):
        batch_index = sections - 1 - section + tick
        seg_wide = lax.dynamic_index_in_dim(seg_all, batch_index, 0, keepdims=False)
        seg_own = seg_wide[sample_lines : 2 * sample_lines]
        resid = present_activity.astype(jnp.float32)
        normed = layer_norm(resid, selfattend_scaling[0]).astype(jnp.bfloat16)
        projected = jnp.dot(normed, full_qkv, preferred_element_type=jnp.float32)
        query = (projected[:, :feature_count] * (feature_count // HEADS) ** (-0.5)).astype(
            jnp.bfloat16
        )
        keys = projected[:, feature_count : 2 * feature_count].astype(jnp.bfloat16)
        values = projected[:, 2 * feature_count :].astype(jnp.bfloat16)
        wide_pairs = extended(jnp.concatenate([keys, values], axis=1), ((FRAME, 0),), sample_lines)
        wide_keys, wide_values = wide_pairs[:, :feature_count], wide_pairs[:, feature_count:]
        context = attend(query, wide_keys, wide_values, seg_wide, seg_own)
        resid = resid + jnp.dot(context, full_out, preferred_element_type=jnp.float32)
        conv_in = layer_norm(resid, depthwise_scaling[0]).astype(jnp.bfloat16)
        doubled = jnp.dot(conv_in, full_glu, preferred_element_type=jnp.float32)
        glu = (doubled[:, :feature_count] * jax.nn.sigmoid(doubled[:, feature_count:])).astype(
            jnp.bfloat16
        )
        wide_glu = extended(glu, ((FRAME, 0),), half)
        depth = depthwise(
            wide_glu,
            seg_wide[sample_lines - half : 2 * sample_lines + half],
            seg_own,
            filter_taps[0],
        )
        act = (depth * jax.nn.sigmoid(depth)).astype(jnp.bfloat16)
        resid = resid + jnp.dot(act, full_mix, preferred_element_type=jnp.float32)
        made = resid.astype(jnp.bfloat16)
        made_all.append(made)
        if tick + 1 < ticks:
            arrived = shifted(made, "section", 1)
            present_activity = jnp.where(section == 0, newcomer_groups[tick], arrived)
    return jnp.stack(made_all)[:, None]


def solution(mesh):
    sections = mesh.shape["section"]
    frames = mesh.shape["frame"]
    mesh = Mesh(mesh.devices.reshape(sections, 2, 4, frames // 8), MESH_AXES)
    in_specs = (
        P(None, FRAME, None),
        P("section", FRAME, None),
        P(None, FRAME),
        P("section", None),
        P("section", FRAME, None),
        P("section", FRAME, None),
        P("section", None),
        P("section", FRAME, None),
        P("section", None, None),
        P("section", FRAME, None),
    )
    out_specs = P(None, "section", FRAME, None)
    return jax.shard_map(
        on_device, mesh=mesh, in_specs=in_specs, out_specs=out_specs, check_vma=False
    )
```

```python
import functools

import jax
import jax.numpy as jnp
from jax import lax
from jax.experimental import pallas as pl
from jax.experimental.pallas import tpu as pltpu
from jax.sharding import Mesh, PartitionSpec as P

HEADS = 24
KERNEL = 31


EPS = 1e-05
FRAME = ("yl", "x", "z")
MESH_AXES = ("section",) + FRAME


def gather_kernel(count, *refs):
    local, gathered = refs[:count], refs[count : 2 * count]
    own_sem, send_sem, recv_sem = refs[2 * count :]
    sizes = {name: lax.axis_size(name) for name in FRAME}
    here = {name: lax.axis_index(name) for name in MESH_AXES}

    def position(coords):
        return (coords["yl"] * sizes["x"] + coords["x"]) * sizes["z"] + coords["z"]

    def moved(coords, name, step):
        if step == 0:
            return coords
        other = dict(coords)
        other[name] = lax.rem(coords[name] + step + sizes[name], sizes[name])
        return other

    neighbours = [moved(here, "yl", 1)]
    for name in ("x", "z"):
        neighbours += [moved(here, name, 1), moved(here, name, -1)]
    barrier = pltpu.get_barrier_semaphore()
    for other in neighbours:
        pl.semaphore_signal(
            barrier, inc=1, device_id=tuple(other[a] for a in MESH_AXES),
            device_id_type=pl.DeviceIdType.MESH,
        )
    pl.semaphore_wait(barrier, len(neighbours))

    own_copies = []
    for w in range(count):
        copy = pltpu.make_async_copy(local[w], gathered[w].at[position(here)], own_sem.at[w])
        copy.start()
        own_copies.append(copy)

    counter = [0]

    def send(w, coords, cols, target):
        index = counter[0]
        counter[0] += 1
        if coords is here:
            source = local[w].at[:, cols]
        else:
            source = gathered[w].at[position(coords), :, cols]
        copy = pltpu.make_async_remote_copy(
            src_ref=source,
            dst_ref=gathered[w].at[position(coords), :, cols],
            send_sem=send_sem.at[index],
            recv_sem=recv_sem.at[index],
            device_id=tuple(target[a] for a in MESH_AXES),
            device_id_type=pl.DeviceIdType.MESH,
        )
        copy.start()
        return copy

    widths = [r.shape[-1] for r in local]
    orders = (("x", "z"), ("z", "x"))
    held = [[[here] for _ in orders] for _ in range(count)]

    def stripe_cols(w, s, part=None):
        half = widths[w] // 2
        lo, width = (0, half) if s == 0 else (half, widths[w] - half)
        if part is None:
            return pl.ds(lo, width)
        quarter = width // 2
        return pl.ds(lo, quarter) if part == 0 else pl.ds(lo + quarter, width - quarter)

    pending = []
    for w in range(count):
        for s in range(len(orders)):
            pending.append(send(w, here, stripe_cols(w, s), moved(here, "yl", 1)))
            held[w][s] = [here, moved(here, "yl", 1)]
    for copy in pending:
        copy.wait()
    for level in range(2):
        pending = []
        for w in range(count):
            for s, order in enumerate(orders):
                name = order[level]
                for coords in held[w][s]:
                    for step in (1, -1):
                        pending.append(send(w, coords, stripe_cols(w, s), moved(here, name, step)))
        for copy in pending:
            copy.wait()
        pending = []
        for w in range(count):
            for s, order in enumerate(orders):
                name = order[level]
                for coords in held[w][s]:
                    pending.append(
                        send(w, moved(coords, name, -1), stripe_cols(w, s, 0), moved(here, name, 1))
                    )
                    pending.append(
                        send(w, moved(coords, name, 1), stripe_cols(w, s, 1), moved(here, name, -1))
                    )
        for copy in pending:
            copy.wait()
        for w in range(count):
            for s, order in enumerate(orders):
                name = order[level]
                held[w][s] = [moved(c, name, step) for c in held[w][s] for step in (0, 1, 2, 3)]
    for copy in own_copies:
        copy.wait()


def gather_weights(blocks):
    count = len(blocks)
    frames = 1
    for name in FRAME:
        frames *= lax.axis_size(name)
    copies = count * 2 * (1 + 2 * (4 + 4 * 4))
    outs = pl.pallas_call(
        functools.partial(gather_kernel, count),
        out_shape=[jax.ShapeDtypeStruct((frames,) + b.shape, b.dtype) for b in blocks],
        in_specs=[pl.BlockSpec(memory_space=pl.ANY)] * count,
        out_specs=[pl.BlockSpec(memory_space=pl.ANY)] * count,
        scratch_shapes=[
            pltpu.SemaphoreType.DMA((count,)),
            pltpu.SemaphoreType.DMA((copies,)),
            pltpu.SemaphoreType.DMA((copies,)),
        ],
        compiler_params=pltpu.CompilerParams(collective_id=0, has_side_effects=True),
    )(*blocks)
    return [o.reshape(frames * o.shape[1], o.shape[2]) for o in outs]


def extended(block, sides, width):
    for axis, dim in sides:
        count = lax.axis_size(axis)
        forward = [(i, i + 1) for i in range(count - 1)]
        backward = [(target, source) for source, target in forward]
        low = lax.ppermute(
            lax.slice_in_dim(block, block.shape[dim] - width, None, axis=dim), axis, forward
        )
        high = lax.ppermute(lax.slice_in_dim(block, 0, width, axis=dim), axis, backward)
        block = jnp.concatenate([low, block, high], axis=dim)
    return block


def shifted(value, axis, steps):
    count = lax.axis_size(axis)
    leading, last = (max(0, -steps), min(count, count - steps))
    return lax.ppermute(value, axis, [(source, source + steps) for source in range(leading, last)])


def relayed(value, step):
    sections, frames = lax.axis_size("section"), lax.axis_size(FRAME)
    pairs = [
        ((source - 1) * frames + frame + step, source * frames + frame)
        for source in range(1, sections)
        for frame in range(frames)
        if 0 <= frame + step < frames
    ]
    return lax.ppermute(value, ("section",) + FRAME, pairs)


def layer_norm(sample_lines, gain):
    mean = jnp.mean(sample_lines, axis=-1, keepdims=True)
    centred = sample_lines - mean
    spread = jnp.mean(centred * centred, axis=-1, keepdims=True)
    return centred * lax.rsqrt(spread + EPS) * gain


def attend(query, wide_keys, wide_values, seg_wide, seg_own):
    sample_lines, feature_count = query.shape
    head_dim = feature_count // HEADS
    shaped_q = query.reshape(sample_lines, HEADS, head_dim)
    shaped_k = wide_keys.reshape(wide_keys.shape[0], HEADS, head_dim)
    shaped_v = wide_values.reshape(wide_values.shape[0], HEADS, head_dim)
    scores = jnp.einsum("qhd,khd->hqk", shaped_q, shaped_k, preferred_element_type=jnp.float32)
    allowed = (seg_own[:, None] == seg_wide[None, :])[None]
    scores = jnp.where(allowed, scores, -1e30)
    top = jnp.max(scores, axis=-1, keepdims=True)
    expd = jnp.exp(scores - top)
    probs = (expd / jnp.sum(expd, axis=-1, keepdims=True)).astype(jnp.bfloat16)
    context = jnp.einsum("hqk,khd->qhd", probs, shaped_v, preferred_element_type=jnp.float32)
    return context.astype(jnp.bfloat16).reshape(sample_lines, feature_count)


def depthwise(wide_glu, seg_conv, seg_own, taps):
    sample_lines = seg_own.shape[0]
    total = jnp.zeros((sample_lines, wide_glu.shape[1]), jnp.float32)
    for tap in range(taps.shape[0]):
        same = (seg_conv[tap : tap + sample_lines] == seg_own)[:, None]
        total = total + jnp.where(
            same, wide_glu[tap : tap + sample_lines].astype(jnp.float32) * taps[tap], 0.0
        )
    return total


def on_device(
    newcomer_groups,
    pending_inputs,
    speaker_clip_ids,
    selfattend_scaling,
    triple_projection_matrix,
    selfattend_final_matrix,
    depthwise_scaling,
    sigmoid_expand_matrix,
    filter_taps,
    combine_channel_matrix,
):
    sample_lines = pending_inputs.shape[1]
    feature_count = pending_inputs.shape[2]
    half = KERNEL // 2
    sections = lax.axis_size("section")
    section = lax.axis_index("section")
    ticks = newcomer_groups.shape[0] + 1
    seg_all = extended(speaker_clip_ids + 1, ((FRAME, 1),), sample_lines)
    full_qkv, full_out, full_glu, full_mix = gather_weights(
        [
            triple_projection_matrix[0],
            selfattend_final_matrix[0],
            sigmoid_expand_matrix[0],
            combine_channel_matrix[0],
        ]
    )
    wide_input = extended(pending_inputs[0], ((FRAME, 0),), sample_lines)
    newcomer_wide = [
        extended(newcomer_groups[tick], ((FRAME, 0),), sample_lines) for tick in range(ticks - 1)
    ]
    made_all = []
    for tick in range(ticks):
        batch_index = sections - 1 - section + tick
        seg_wide = lax.dynamic_index_in_dim(seg_all, batch_index, 0, keepdims=False)
        seg_own = seg_wide[sample_lines : 2 * sample_lines]
        resid_wide = wide_input.astype(jnp.float32)
        normed = layer_norm(resid_wide, selfattend_scaling[0]).astype(jnp.bfloat16)
        projected = jnp.dot(normed, full_qkv, preferred_element_type=jnp.float32)
        query = (
            projected[sample_lines : 2 * sample_lines, :feature_count]
            * (feature_count // HEADS) ** (-0.5)
        ).astype(jnp.bfloat16)
        wide_keys = projected[:, feature_count : 2 * feature_count].astype(jnp.bfloat16)
        wide_values = projected[:, 2 * feature_count :].astype(jnp.bfloat16)
        resid = resid_wide[sample_lines : 2 * sample_lines]
        context = attend(query, wide_keys, wide_values, seg_wide, seg_own)
        resid = resid + jnp.dot(context, full_out, preferred_element_type=jnp.float32)
        conv_in = layer_norm(resid, depthwise_scaling[0]).astype(jnp.bfloat16)
        doubled = jnp.dot(conv_in, full_glu, preferred_element_type=jnp.float32)
        glu = (doubled[:, :feature_count] * jax.nn.sigmoid(doubled[:, feature_count:])).astype(
            jnp.bfloat16
        )
        wide_glu = extended(glu, ((FRAME, 0),), half)
        depth = depthwise(
            wide_glu,
            seg_wide[sample_lines - half : 2 * sample_lines + half],
            seg_own,
            filter_taps[0],
        )
        act = (depth * jax.nn.sigmoid(depth)).astype(jnp.bfloat16)
        resid = resid + jnp.dot(act, full_mix, preferred_element_type=jnp.float32)
        made = resid.astype(jnp.bfloat16)
        made_all.append(made)
        if tick + 1 < ticks:
            arrived = jnp.concatenate([relayed(made, step) for step in (-1, 0, 1)], axis=0)
            wide_input = jnp.where(section == 0, newcomer_wide[tick], arrived)
    return jnp.stack(made_all)[:, None]


def solution(mesh):
    sections = mesh.shape["section"]
    frames = mesh.shape["frame"]
    mesh = Mesh(mesh.devices.reshape(sections, 2, 4, frames // 8), MESH_AXES)
    in_specs = (
        P(None, FRAME, None),
        P("section", FRAME, None),
        P(None, FRAME),
        P("section", None),
        P("section", FRAME, None),
        P("section", FRAME, None),
        P("section", None),
        P("section", FRAME, None),
        P("section", None, None),
        P("section", FRAME, None),
    )
    out_specs = P(None, "section", FRAME, None)
    return jax.shard_map(
        on_device, mesh=mesh, in_specs=in_specs, out_specs=out_specs, check_vma=False
    )
```

```python
import functools

import jax
import jax.numpy as jnp
from jax import lax
from jax.experimental import pallas as pl
from jax.experimental.pallas import tpu as pltpu
from jax.sharding import Mesh, PartitionSpec as P

HEADS = 24
KERNEL = 31


EPS = 1e-05
FRAME = ("yl", "x", "z")
MESH_AXES = ("section",) + FRAME


def gather_kernel(count, *refs):
    local, gathered = refs[:count], refs[count : 2 * count]
    own_sem, send_sem, recv_sem = refs[2 * count :]
    sizes = {name: lax.axis_size(name) for name in FRAME}
    here = {name: lax.axis_index(name) for name in MESH_AXES}

    def position(coords):
        return (coords["yl"] * sizes["x"] + coords["x"]) * sizes["z"] + coords["z"]

    def moved(coords, name, step):
        if step == 0:
            return coords
        other = dict(coords)
        other[name] = lax.rem(coords[name] + step + sizes[name], sizes[name])
        return other

    neighbours = [moved(here, "yl", 1)]
    for name in ("x", "z"):
        neighbours += [moved(here, name, 1), moved(here, name, -1)]
    barrier = pltpu.get_barrier_semaphore()
    for other in neighbours:
        pl.semaphore_signal(
            barrier, inc=1, device_id=tuple(other[a] for a in MESH_AXES),
            device_id_type=pl.DeviceIdType.MESH,
        )
    pl.semaphore_wait(barrier, len(neighbours))

    own_copies = []
    for w in range(count):
        copy = pltpu.make_async_copy(local[w], gathered[w].at[position(here)], own_sem.at[w])
        copy.start()
        own_copies.append(copy)

    counter = [0]

    def send(w, coords, cols, target):
        index = counter[0]
        counter[0] += 1
        if coords is here:
            source = local[w].at[:, cols]
        else:
            source = gathered[w].at[position(coords), :, cols]
        copy = pltpu.make_async_remote_copy(
            src_ref=source,
            dst_ref=gathered[w].at[position(coords), :, cols],
            send_sem=send_sem.at[index],
            recv_sem=recv_sem.at[index],
            device_id=tuple(target[a] for a in MESH_AXES),
            device_id_type=pl.DeviceIdType.MESH,
        )
        copy.start()
        return copy

    widths = [r.shape[-1] for r in local]
    orders = (("x", "z"), ("z", "x"))
    held = [[[here] for _ in orders] for _ in range(count)]

    def stripe_cols(w, s, part=None):
        half = widths[w] // 2
        lo, width = (0, half) if s == 0 else (half, widths[w] - half)
        if part is None:
            return pl.ds(lo, width)
        quarter = width // 2
        return pl.ds(lo, quarter) if part == 0 else pl.ds(lo + quarter, width - quarter)

    pending = []
    for w in range(count):
        for s in range(len(orders)):
            pending.append(send(w, here, stripe_cols(w, s), moved(here, "yl", 1)))
            held[w][s] = [here, moved(here, "yl", 1)]
    for copy in pending:
        copy.wait()
    for level in range(2):
        pending = []
        for w in range(count):
            for s, order in enumerate(orders):
                name = order[level]
                for coords in held[w][s]:
                    for step in (1, -1):
                        pending.append(send(w, coords, stripe_cols(w, s), moved(here, name, step)))
        for copy in pending:
            copy.wait()
        pending = []
        for w in range(count):
            for s, order in enumerate(orders):
                name = order[level]
                for coords in held[w][s]:
                    pending.append(
                        send(w, moved(coords, name, -1), stripe_cols(w, s, 0), moved(here, name, 1))
                    )
                    pending.append(
                        send(w, moved(coords, name, 1), stripe_cols(w, s, 1), moved(here, name, -1))
                    )
        for copy in pending:
            copy.wait()
        for w in range(count):
            for s, order in enumerate(orders):
                name = order[level]
                held[w][s] = [moved(c, name, step) for c in held[w][s] for step in (0, 1, 2, 3)]
    for copy in own_copies:
        copy.wait()


def gather_weights(blocks):
    count = len(blocks)
    frames = 1
    for name in FRAME:
        frames *= lax.axis_size(name)
    copies = count * 2 * (1 + 2 * (4 + 4 * 4))
    outs = pl.pallas_call(
        functools.partial(gather_kernel, count),
        out_shape=[jax.ShapeDtypeStruct((frames,) + b.shape, b.dtype) for b in blocks],
        in_specs=[pl.BlockSpec(memory_space=pl.ANY)] * count,
        out_specs=[pl.BlockSpec(memory_space=pl.ANY)] * count,
        scratch_shapes=[
            pltpu.SemaphoreType.DMA((count,)),
            pltpu.SemaphoreType.DMA((copies,)),
            pltpu.SemaphoreType.DMA((copies,)),
        ],
        compiler_params=pltpu.CompilerParams(collective_id=0, has_side_effects=True),
    )(*blocks)
    return [o.reshape(frames * o.shape[1], o.shape[2]) for o in outs]


def extended(block, sides, width):
    for axis, dim in sides:
        count = lax.axis_size(axis)
        forward = [(i, i + 1) for i in range(count - 1)]
        backward = [(target, source) for source, target in forward]
        low = lax.ppermute(
            lax.slice_in_dim(block, block.shape[dim] - width, None, axis=dim), axis, forward
        )
        high = lax.ppermute(lax.slice_in_dim(block, 0, width, axis=dim), axis, backward)
        block = jnp.concatenate([low, block, high], axis=dim)
    return block


def shifted(value, axis, steps):
    count = lax.axis_size(axis)
    leading, last = (max(0, -steps), min(count, count - steps))
    return lax.ppermute(value, axis, [(source, source + steps) for source in range(leading, last)])


def layer_norm(sample_lines, gain):
    mean = jnp.mean(sample_lines, axis=-1, keepdims=True)
    centred = sample_lines - mean
    spread = jnp.mean(centred * centred, axis=-1, keepdims=True)
    return centred * lax.rsqrt(spread + EPS) * gain


def attend(query, wide_keys, wide_values, seg_wide, seg_own):
    sample_lines, feature_count = query.shape
    head_dim = feature_count // HEADS
    shaped_q = query.reshape(sample_lines, HEADS, head_dim)
    shaped_k = wide_keys.reshape(wide_keys.shape[0], HEADS, head_dim)
    shaped_v = wide_values.reshape(wide_values.shape[0], HEADS, head_dim)
    scores = jnp.einsum("qhd,khd->hqk", shaped_q, shaped_k, preferred_element_type=jnp.float32)
    allowed = (seg_own[:, None] == seg_wide[None, :])[None]
    scores = jnp.where(allowed, scores, -1e30)
    top = jnp.max(scores, axis=-1, keepdims=True)
    expd = jnp.exp(scores - top)
    probs = (expd / jnp.sum(expd, axis=-1, keepdims=True)).astype(jnp.bfloat16)
    context = jnp.einsum("hqk,khd->qhd", probs, shaped_v, preferred_element_type=jnp.float32)
    return context.astype(jnp.bfloat16).reshape(sample_lines, feature_count)


def attention_kernel(head_dim, q_ref, segq_ref, segk_ref, *refs):
    keys, values, out_ref = refs[:3], refs[3:6], refs[6]
    own = segq_ref[...]
    masks = [own == segk_ref[b] for b in range(3)]
    for head in range(q_ref.shape[1] // head_dim):
        cols = slice(head * head_dim, (head + 1) * head_dim)
        query = q_ref[:, cols]
        scores = [
            jnp.where(
                masks[b],
                lax.dot_general(
                    query, keys[b][:, cols], (((1,), (1,)), ((), ())),
                    preferred_element_type=jnp.float32,
                ),
                -1e30,
            )
            for b in range(3)
        ]
        top = jnp.maximum(
            jnp.maximum(jnp.max(scores[0], axis=1, keepdims=True), jnp.max(scores[1], axis=1, keepdims=True)),
            jnp.max(scores[2], axis=1, keepdims=True),
        )
        expd = [jnp.exp(s - top) for s in scores]
        total = (
            jnp.sum(expd[0], axis=1, keepdims=True)
            + jnp.sum(expd[1], axis=1, keepdims=True)
            + jnp.sum(expd[2], axis=1, keepdims=True)
        )
        context = None
        for b in range(3):
            probs = (expd[b] / total).astype(jnp.bfloat16)
            part = jnp.dot(probs, values[b][:, cols], preferred_element_type=jnp.float32)
            context = part if context is None else context + part
        out_ref[:, cols] = context.astype(out_ref.dtype)


def attend_blocks(query, key_blocks, value_blocks, seg_wide, seg_own):
    lines, width = query.shape
    head_dim = width // HEADS
    step = 2 * head_dim
    tile = pl.BlockSpec((lines, step), lambda j: (0, j))
    return pl.pallas_call(
        functools.partial(attention_kernel, head_dim),
        out_shape=jax.ShapeDtypeStruct((lines, width), jnp.bfloat16),
        grid=(width // step,),
        in_specs=[
            tile,
            pl.BlockSpec((lines, 1), lambda j: (0, 0)),
            pl.BlockSpec((3, 1, lines), lambda j: (0, 0, 0)),
        ]
        + [tile] * 6,
        out_specs=tile,
        cost_estimate=pl.CostEstimate(
            flops=4 * lines * 3 * lines * width,
            transcendentals=HEADS * lines * 3 * lines,
            bytes_accessed=7 * lines * width * 2 + lines * width * 2,
        ),
    )(
        query,
        seg_own.reshape(lines, 1),
        seg_wide.reshape(3, 1, lines),
        *key_blocks,
        *value_blocks,
    )


def halo_blocks(block, axis):
    count = lax.axis_size(axis)
    forward = [(i, i + 1) for i in range(count - 1)]
    backward = [(target, source) for source, target in forward]
    return lax.ppermute(block, axis, forward), block, lax.ppermute(block, axis, backward)


def depthwise(wide_glu, seg_conv, seg_own, taps):
    sample_lines = seg_own.shape[0]
    total = jnp.zeros((sample_lines, wide_glu.shape[1]), jnp.float32)
    for tap in range(taps.shape[0]):
        same = (seg_conv[tap : tap + sample_lines] == seg_own)[:, None]
        total = total + jnp.where(
            same, wide_glu[tap : tap + sample_lines].astype(jnp.float32) * taps[tap], 0.0
        )
    return total


def on_device(
    newcomer_groups,
    pending_inputs,
    speaker_clip_ids,
    selfattend_scaling,
    triple_projection_matrix,
    selfattend_final_matrix,
    depthwise_scaling,
    sigmoid_expand_matrix,
    filter_taps,
    combine_channel_matrix,
):
    sample_lines = pending_inputs.shape[1]
    feature_count = pending_inputs.shape[2]
    half = KERNEL // 2
    sections = lax.axis_size("section")
    section = lax.axis_index("section")
    ticks = newcomer_groups.shape[0] + 1
    seg_all = extended(speaker_clip_ids + 1, ((FRAME, 1),), sample_lines)
    full_qkv, full_out, full_glu, full_mix = gather_weights(
        [
            triple_projection_matrix[0],
            selfattend_final_matrix[0],
            sigmoid_expand_matrix[0],
            combine_channel_matrix[0],
        ]
    )
    present_activity = pending_inputs[0]
    made_all = []
    for tick in range(ticks):
        batch_index = sections - 1 - section + tick
        seg_wide = lax.dynamic_index_in_dim(seg_all, batch_index, 0, keepdims=False)
        seg_own = seg_wide[sample_lines : 2 * sample_lines]
        resid = present_activity.astype(jnp.float32)
        normed = layer_norm(resid, selfattend_scaling[0]).astype(jnp.bfloat16)
        projected = jnp.dot(normed, full_qkv, preferred_element_type=jnp.float32)
        query = (projected[:, :feature_count] * (feature_count // HEADS) ** (-0.5)).astype(
            jnp.bfloat16
        )
        keys = projected[:, feature_count : 2 * feature_count].astype(jnp.bfloat16)
        values = projected[:, 2 * feature_count :].astype(jnp.bfloat16)
        context = attend_blocks(
            query, halo_blocks(keys, FRAME), halo_blocks(values, FRAME), seg_wide, seg_own
        )
        resid = resid + jnp.dot(context, full_out, preferred_element_type=jnp.float32)
        conv_in = layer_norm(resid, depthwise_scaling[0]).astype(jnp.bfloat16)
        doubled = jnp.dot(conv_in, full_glu, preferred_element_type=jnp.float32)
        glu = (doubled[:, :feature_count] * jax.nn.sigmoid(doubled[:, feature_count:])).astype(
            jnp.bfloat16
        )
        wide_glu = extended(glu, ((FRAME, 0),), half)
        depth = depthwise(
            wide_glu,
            seg_wide[sample_lines - half : 2 * sample_lines + half],
            seg_own,
            filter_taps[0],
        )
        act = (depth * jax.nn.sigmoid(depth)).astype(jnp.bfloat16)
        resid = resid + jnp.dot(act, full_mix, preferred_element_type=jnp.float32)
        made = resid.astype(jnp.bfloat16)
        made_all.append(made)
        if tick + 1 < ticks:
            arrived = shifted(made, "section", 1)
            present_activity = jnp.where(section == 0, newcomer_groups[tick], arrived)
    return jnp.stack(made_all)[:, None]


def solution(mesh):
    sections = mesh.shape["section"]
    frames = mesh.shape["frame"]
    mesh = Mesh(mesh.devices.reshape(sections, 2, 4, frames // 8), MESH_AXES)
    in_specs = (
        P(None, FRAME, None),
        P("section", FRAME, None),
        P(None, FRAME),
        P("section", None),
        P("section", FRAME, None),
        P("section", FRAME, None),
        P("section", None),
        P("section", FRAME, None),
        P("section", None, None),
        P("section", FRAME, None),
    )
    out_specs = P(None, "section", FRAME, None)
    return jax.shard_map(
        on_device, mesh=mesh, in_specs=in_specs, out_specs=out_specs, check_vma=False
    )
```

```python
import functools

import jax
import jax.numpy as jnp
from jax import lax
from jax.experimental import pallas as pl
from jax.experimental.pallas import tpu as pltpu
from jax.sharding import Mesh, PartitionSpec as P

HEADS = 24
KERNEL = 31


EPS = 1e-05
FRAME = ("yl", "x", "z")
MESH_AXES = ("section",) + FRAME


def gather_kernel(count, *refs):
    local, gathered = refs[:count], refs[count : 2 * count]
    own_sem, send_sem, recv_sem = refs[2 * count :]
    sizes = {name: lax.axis_size(name) for name in FRAME}
    here = {name: lax.axis_index(name) for name in MESH_AXES}

    def position(coords):
        return (coords["yl"] * sizes["x"] + coords["x"]) * sizes["z"] + coords["z"]

    def moved(coords, name, step):
        if step == 0:
            return coords
        other = dict(coords)
        other[name] = lax.rem(coords[name] + step + sizes[name], sizes[name])
        return other

    neighbours = [moved(here, "yl", 1)]
    for name in ("x", "z"):
        neighbours += [moved(here, name, 1), moved(here, name, -1)]
    barrier = pltpu.get_barrier_semaphore()
    for other in neighbours:
        pl.semaphore_signal(
            barrier, inc=1, device_id=tuple(other[a] for a in MESH_AXES),
            device_id_type=pl.DeviceIdType.MESH,
        )
    pl.semaphore_wait(barrier, len(neighbours))

    own_copies = []
    for w in range(count):
        copy = pltpu.make_async_copy(local[w], gathered[w].at[position(here)], own_sem.at[w])
        copy.start()
        own_copies.append(copy)

    counter = [0]

    def send(w, coords, cols, target):
        index = counter[0]
        counter[0] += 1
        if coords is here:
            source = local[w].at[:, cols]
        else:
            source = gathered[w].at[position(coords), :, cols]
        copy = pltpu.make_async_remote_copy(
            src_ref=source,
            dst_ref=gathered[w].at[position(coords), :, cols],
            send_sem=send_sem.at[index],
            recv_sem=recv_sem.at[index],
            device_id=tuple(target[a] for a in MESH_AXES),
            device_id_type=pl.DeviceIdType.MESH,
        )
        copy.start()
        return copy

    widths = [r.shape[-1] for r in local]
    orders = (("x", "z"), ("z", "x"))
    held = [[[here] for _ in orders] for _ in range(count)]

    def stripe_cols(w, s, part=None):
        half = widths[w] // 2
        lo, width = (0, half) if s == 0 else (half, widths[w] - half)
        if part is None:
            return pl.ds(lo, width)
        quarter = width // 2
        return pl.ds(lo, quarter) if part == 0 else pl.ds(lo + quarter, width - quarter)

    pending = []
    for w in range(count):
        for s in range(len(orders)):
            pending.append(send(w, here, stripe_cols(w, s), moved(here, "yl", 1)))
            held[w][s] = [here, moved(here, "yl", 1)]
    for copy in pending:
        copy.wait()
    for level in range(2):
        pending = []
        for w in range(count):
            for s, order in enumerate(orders):
                name = order[level]
                for coords in held[w][s]:
                    for step in (1, -1):
                        pending.append(send(w, coords, stripe_cols(w, s), moved(here, name, step)))
        for copy in pending:
            copy.wait()
        pending = []
        for w in range(count):
            for s, order in enumerate(orders):
                name = order[level]
                for coords in held[w][s]:
                    pending.append(
                        send(w, moved(coords, name, -1), stripe_cols(w, s, 0), moved(here, name, 1))
                    )
                    pending.append(
                        send(w, moved(coords, name, 1), stripe_cols(w, s, 1), moved(here, name, -1))
                    )
        for copy in pending:
            copy.wait()
        for w in range(count):
            for s, order in enumerate(orders):
                name = order[level]
                held[w][s] = [moved(c, name, step) for c in held[w][s] for step in (0, 1, 2, 3)]
    for copy in own_copies:
        copy.wait()


def gather_weights(blocks):
    count = len(blocks)
    frames = 1
    for name in FRAME:
        frames *= lax.axis_size(name)
    copies = count * 2 * (1 + 2 * (4 + 4 * 4))
    outs = pl.pallas_call(
        functools.partial(gather_kernel, count),
        out_shape=[jax.ShapeDtypeStruct((frames,) + b.shape, b.dtype) for b in blocks],
        in_specs=[pl.BlockSpec(memory_space=pl.ANY)] * count,
        out_specs=[pl.BlockSpec(memory_space=pl.ANY)] * count,
        scratch_shapes=[
            pltpu.SemaphoreType.DMA((count,)),
            pltpu.SemaphoreType.DMA((copies,)),
            pltpu.SemaphoreType.DMA((copies,)),
        ],
        compiler_params=pltpu.CompilerParams(collective_id=0, has_side_effects=True),
    )(*blocks)
    return [o.reshape(frames * o.shape[1], o.shape[2]) for o in outs]


def extended(block, sides, width):
    for axis, dim in sides:
        count = lax.axis_size(axis)
        forward = [(i, i + 1) for i in range(count - 1)]
        backward = [(target, source) for source, target in forward]
        low = lax.ppermute(
            lax.slice_in_dim(block, block.shape[dim] - width, None, axis=dim), axis, forward
        )
        high = lax.ppermute(lax.slice_in_dim(block, 0, width, axis=dim), axis, backward)
        block = jnp.concatenate([low, block, high], axis=dim)
    return block


def shifted(value, axis, steps):
    count = lax.axis_size(axis)
    leading, last = (max(0, -steps), min(count, count - steps))
    return lax.ppermute(value, axis, [(source, source + steps) for source in range(leading, last)])


def layer_norm(sample_lines, gain):
    mean = jnp.mean(sample_lines, axis=-1, keepdims=True)
    centred = sample_lines - mean
    spread = jnp.mean(centred * centred, axis=-1, keepdims=True)
    return centred * lax.rsqrt(spread + EPS) * gain


def attend(query, wide_keys, wide_values, seg_wide, seg_own):
    sample_lines, feature_count = query.shape
    head_dim = feature_count // HEADS
    shaped_q = query.reshape(sample_lines, HEADS, head_dim)
    shaped_k = wide_keys.reshape(wide_keys.shape[0], HEADS, head_dim)
    shaped_v = wide_values.reshape(wide_values.shape[0], HEADS, head_dim)
    scores = jnp.einsum("qhd,khd->hqk", shaped_q, shaped_k, preferred_element_type=jnp.float32)
    allowed = (seg_own[:, None] == seg_wide[None, :])[None]
    scores = jnp.where(allowed, scores, -1e30)
    top = jnp.max(scores, axis=-1, keepdims=True)
    expd = jnp.exp(scores - top)
    probs = (expd / jnp.sum(expd, axis=-1, keepdims=True)).astype(jnp.bfloat16)
    context = jnp.einsum("hqk,khd->qhd", probs, shaped_v, preferred_element_type=jnp.float32)
    return context.astype(jnp.bfloat16).reshape(sample_lines, feature_count)


def conv_kernel(glu_ref, segc_ref, sego_ref, taps_ref, out_ref):
    lines = out_ref.shape[0]
    own = sego_ref[...]
    total = jnp.zeros(out_ref.shape, jnp.float32)
    for tap in range(taps_ref.shape[0]):
        same = segc_ref[pl.ds(tap, lines), :] == own
        window = glu_ref[pl.ds(tap, lines), :]
        total = total + jnp.where(same, window * taps_ref[pl.ds(tap, 1), :], 0.0)
    out_ref[...] = (total * jax.nn.sigmoid(total)).astype(out_ref.dtype)


def depthwise_act(wide_glu, seg_conv, seg_own, taps):
    lines = seg_own.shape[0]
    rows, width = wide_glu.shape
    step = 512
    return pl.pallas_call(
        conv_kernel,
        out_shape=jax.ShapeDtypeStruct((lines, width), jnp.bfloat16),
        grid=(width // step,),
        in_specs=[
            pl.BlockSpec((rows, step), lambda j: (0, j)),
            pl.BlockSpec((rows, 1), lambda j: (0, 0)),
            pl.BlockSpec((lines, 1), lambda j: (0, 0)),
            pl.BlockSpec((taps.shape[0], step), lambda j: (0, j)),
        ],
        out_specs=pl.BlockSpec((lines, step), lambda j: (0, j)),
        cost_estimate=pl.CostEstimate(
            flops=3 * taps.shape[0] * lines * width,
            transcendentals=lines * width,
            bytes_accessed=rows * width * 4 + lines * width * 2,
        ),
    )(wide_glu.astype(jnp.float32), seg_conv.reshape(rows, 1), seg_own.reshape(lines, 1), taps)


def depthwise(wide_glu, seg_conv, seg_own, taps):
    sample_lines = seg_own.shape[0]
    total = jnp.zeros((sample_lines, wide_glu.shape[1]), jnp.float32)
    for tap in range(taps.shape[0]):
        same = (seg_conv[tap : tap + sample_lines] == seg_own)[:, None]
        total = total + jnp.where(
            same, wide_glu[tap : tap + sample_lines].astype(jnp.float32) * taps[tap], 0.0
        )
    return total


def on_device(
    newcomer_groups,
    pending_inputs,
    speaker_clip_ids,
    selfattend_scaling,
    triple_projection_matrix,
    selfattend_final_matrix,
    depthwise_scaling,
    sigmoid_expand_matrix,
    filter_taps,
    combine_channel_matrix,
):
    sample_lines = pending_inputs.shape[1]
    feature_count = pending_inputs.shape[2]
    half = KERNEL // 2
    sections = lax.axis_size("section")
    section = lax.axis_index("section")
    ticks = newcomer_groups.shape[0] + 1
    seg_all = extended(speaker_clip_ids + 1, ((FRAME, 1),), sample_lines)
    full_qkv, full_out, full_glu, full_mix = gather_weights(
        [
            triple_projection_matrix[0],
            selfattend_final_matrix[0],
            sigmoid_expand_matrix[0],
            combine_channel_matrix[0],
        ]
    )
    present_activity = pending_inputs[0]
    made_all = []
    for tick in range(ticks):
        batch_index = sections - 1 - section + tick
        seg_wide = lax.dynamic_index_in_dim(seg_all, batch_index, 0, keepdims=False)
        seg_own = seg_wide[sample_lines : 2 * sample_lines]
        resid = present_activity.astype(jnp.float32)
        normed = layer_norm(resid, selfattend_scaling[0]).astype(jnp.bfloat16)
        projected = jnp.dot(normed, full_qkv, preferred_element_type=jnp.float32)
        query = (projected[:, :feature_count] * (feature_count // HEADS) ** (-0.5)).astype(
            jnp.bfloat16
        )
        keys = projected[:, feature_count : 2 * feature_count].astype(jnp.bfloat16)
        values = projected[:, 2 * feature_count :].astype(jnp.bfloat16)
        wide_keys, wide_values = (
            extended(keys, ((FRAME, 0),), sample_lines),
            extended(values, ((FRAME, 0),), sample_lines),
        )
        context = attend(query, wide_keys, wide_values, seg_wide, seg_own)
        resid = resid + jnp.dot(context, full_out, preferred_element_type=jnp.float32)
        conv_in = layer_norm(resid, depthwise_scaling[0]).astype(jnp.bfloat16)
        doubled = jnp.dot(conv_in, full_glu, preferred_element_type=jnp.float32)
        glu = (doubled[:, :feature_count] * jax.nn.sigmoid(doubled[:, feature_count:])).astype(
            jnp.bfloat16
        )
        wide_glu = extended(glu, ((FRAME, 0),), half)
        act = depthwise_act(
            wide_glu,
            seg_wide[sample_lines - half : 2 * sample_lines + half],
            seg_own,
            filter_taps[0],
        )
        resid = resid + jnp.dot(act, full_mix, preferred_element_type=jnp.float32)
        made = resid.astype(jnp.bfloat16)
        made_all.append(made)
        if tick + 1 < ticks:
            arrived = shifted(made, "section", 1)
            present_activity = jnp.where(section == 0, newcomer_groups[tick], arrived)
    return jnp.stack(made_all)[:, None]


def solution(mesh):
    sections = mesh.shape["section"]
    frames = mesh.shape["frame"]
    mesh = Mesh(mesh.devices.reshape(sections, 2, 4, frames // 8), MESH_AXES)
    in_specs = (
        P(None, FRAME, None),
        P("section", FRAME, None),
        P(None, FRAME),
        P("section", None),
        P("section", FRAME, None),
        P("section", FRAME, None),
        P("section", None),
        P("section", FRAME, None),
        P("section", None, None),
        P("section", FRAME, None),
    )
    out_specs = P(None, "section", FRAME, None)
    return jax.shard_map(
        on_device, mesh=mesh, in_specs=in_specs, out_specs=out_specs, check_vma=False
    )
```

```python
import functools

import jax
import jax.numpy as jnp
from jax import lax
from jax.experimental import pallas as pl
from jax.experimental.pallas import tpu as pltpu
from jax.sharding import Mesh, PartitionSpec as P

HEADS = 24
KERNEL = 31


EPS = 1e-05
FRAME = ("yl", "x", "z")
MESH_AXES = ("section",) + FRAME


ORDERS = (("yl", "x", "z"), ("yl", "z", "x"), ("x", "z", "yl"), ("z", "x", "yl"))
LANES = 128


def stripe_plan(width):
    tiles = width // LANES
    late = max(1, round(tiles * 0.14))
    early = (tiles - 2 * late) // 2
    counts = (early, tiles - 2 * late - early, late, late)
    plan, lo = [], 0
    for n in counts:
        first = n // 2
        plan.append((lo * LANES, (first * LANES, (n - first) * LANES)))
        lo += n
    return plan


def copy_count(count):
    sizes = {"yl": 2, "x": 4, "z": 4}
    total = 0
    for order in ORDERS:
        held = 1
        for name in order:
            total += held if sizes[name] == 2 else 4 * held
            held *= sizes[name]
    return count * total


def gather_kernel(count, *refs):
    local, gathered = refs[:count], refs[count : 2 * count]
    own_sem, send_sem, recv_sem = refs[2 * count :]
    sizes = {name: lax.axis_size(name) for name in FRAME}
    here = {name: lax.axis_index(name) for name in MESH_AXES}

    def position(coords):
        return (coords["yl"] * sizes["x"] + coords["x"]) * sizes["z"] + coords["z"]

    def moved(coords, name, step):
        if step == 0:
            return coords
        other = dict(coords)
        other[name] = lax.rem(coords[name] + step + sizes[name], sizes[name])
        return other

    neighbours = [moved(here, "yl", 1)]
    for name in ("x", "z"):
        neighbours += [moved(here, name, 1), moved(here, name, -1)]
    barrier = pltpu.get_barrier_semaphore()
    for other in neighbours:
        pl.semaphore_signal(
            barrier, inc=1, device_id=tuple(other[a] for a in MESH_AXES),
            device_id_type=pl.DeviceIdType.MESH,
        )
    pl.semaphore_wait(barrier, len(neighbours))

    own_copies = []
    for w in range(count):
        copy = pltpu.make_async_copy(local[w], gathered[w].at[position(here)], own_sem.at[w])
        copy.start()
        own_copies.append(copy)

    counter = [0]

    def send(w, coords, cols, target):
        index = counter[0]
        counter[0] += 1
        if coords is here:
            source = local[w].at[:, cols]
        else:
            source = gathered[w].at[position(coords), :, cols]
        copy = pltpu.make_async_remote_copy(
            src_ref=source,
            dst_ref=gathered[w].at[position(coords), :, cols],
            send_sem=send_sem.at[index],
            recv_sem=recv_sem.at[index],
            device_id=tuple(target[a] for a in MESH_AXES),
            device_id_type=pl.DeviceIdType.MESH,
        )
        copy.start()
        return copy

    plans = [stripe_plan(r.shape[-1]) for r in local]
    held = [[[here] for _ in ORDERS] for _ in range(count)]
    for level in range(len(FRAME)):
        for forward in (False, True):
            pending = []
            for w in range(count):
                for s, order in enumerate(ORDERS):
                    name = order[level]
                    if forward and sizes[name] == 2:
                        continue
                    lo, halves = plans[w][s]
                    for coords in held[w][s]:
                        if not forward:
                            whole = pl.ds(lo, halves[0] + halves[1])
                            for step in (1, -1)[: sizes[name] - 2 if sizes[name] > 2 else 1]:
                                pending.append(send(w, coords, whole, moved(here, name, step)))
                        else:
                            first = pl.ds(lo, halves[0])
                            second = pl.ds(lo + halves[0], halves[1])
                            pending.append(
                                send(w, moved(coords, name, -1), first, moved(here, name, 1))
                            )
                            pending.append(
                                send(w, moved(coords, name, 1), second, moved(here, name, -1))
                            )
            for copy in pending:
                copy.wait()
        for w in range(count):
            for s, order in enumerate(ORDERS):
                name = order[level]
                held[w][s] = [moved(c, name, step) for c in held[w][s] for step in range(sizes[name])]
    for copy in own_copies:
        copy.wait()


def gather_weights(blocks):
    count = len(blocks)
    frames = 1
    for name in FRAME:
        frames *= lax.axis_size(name)
    copies = copy_count(count)
    outs = pl.pallas_call(
        functools.partial(gather_kernel, count),
        out_shape=[jax.ShapeDtypeStruct((frames,) + b.shape, b.dtype) for b in blocks],
        in_specs=[pl.BlockSpec(memory_space=pl.ANY)] * count,
        out_specs=[pl.BlockSpec(memory_space=pl.ANY)] * count,
        scratch_shapes=[
            pltpu.SemaphoreType.DMA((count,)),
            pltpu.SemaphoreType.DMA((copies,)),
            pltpu.SemaphoreType.DMA((copies,)),
        ],
        compiler_params=pltpu.CompilerParams(collective_id=0, has_side_effects=True),
    )(*blocks)
    return [o.reshape(frames * o.shape[1], o.shape[2]) for o in outs]


def extended(block, sides, width):
    for axis, dim in sides:
        count = lax.axis_size(axis)
        forward = [(i, i + 1) for i in range(count - 1)]
        backward = [(target, source) for source, target in forward]
        low = lax.ppermute(
            lax.slice_in_dim(block, block.shape[dim] - width, None, axis=dim), axis, forward
        )
        high = lax.ppermute(lax.slice_in_dim(block, 0, width, axis=dim), axis, backward)
        block = jnp.concatenate([low, block, high], axis=dim)
    return block


def shifted(value, axis, steps):
    count = lax.axis_size(axis)
    leading, last = (max(0, -steps), min(count, count - steps))
    return lax.ppermute(value, axis, [(source, source + steps) for source in range(leading, last)])


def layer_norm(sample_lines, gain):
    mean = jnp.mean(sample_lines, axis=-1, keepdims=True)
    centred = sample_lines - mean
    spread = jnp.mean(centred * centred, axis=-1, keepdims=True)
    return centred * lax.rsqrt(spread + EPS) * gain


def attend(query, wide_keys, wide_values, seg_wide, seg_own):
    sample_lines, feature_count = query.shape
    head_dim = feature_count // HEADS
    shaped_q = query.reshape(sample_lines, HEADS, head_dim)
    shaped_k = wide_keys.reshape(wide_keys.shape[0], HEADS, head_dim)
    shaped_v = wide_values.reshape(wide_values.shape[0], HEADS, head_dim)
    scores = jnp.einsum("qhd,khd->hqk", shaped_q, shaped_k, preferred_element_type=jnp.float32)
    allowed = (seg_own[:, None] == seg_wide[None, :])[None]
    scores = jnp.where(allowed, scores, -1e30)
    top = jnp.max(scores, axis=-1, keepdims=True)
    expd = jnp.exp(scores - top)
    probs = (expd / jnp.sum(expd, axis=-1, keepdims=True)).astype(jnp.bfloat16)
    context = jnp.einsum("hqk,khd->qhd", probs, shaped_v, preferred_element_type=jnp.float32)
    return context.astype(jnp.bfloat16).reshape(sample_lines, feature_count)


def depthwise(wide_glu, seg_conv, seg_own, taps):
    sample_lines = seg_own.shape[0]
    total = jnp.zeros((sample_lines, wide_glu.shape[1]), jnp.float32)
    for tap in range(taps.shape[0]):
        same = (seg_conv[tap : tap + sample_lines] == seg_own)[:, None]
        total = total + jnp.where(
            same, wide_glu[tap : tap + sample_lines].astype(jnp.float32) * taps[tap], 0.0
        )
    return total


def on_device(
    newcomer_groups,
    pending_inputs,
    speaker_clip_ids,
    selfattend_scaling,
    triple_projection_matrix,
    selfattend_final_matrix,
    depthwise_scaling,
    sigmoid_expand_matrix,
    filter_taps,
    combine_channel_matrix,
):
    sample_lines = pending_inputs.shape[1]
    feature_count = pending_inputs.shape[2]
    half = KERNEL // 2
    sections = lax.axis_size("section")
    section = lax.axis_index("section")
    ticks = newcomer_groups.shape[0] + 1
    seg_all = extended(speaker_clip_ids + 1, ((FRAME, 1),), sample_lines)
    full_qkv, full_out, full_glu, full_mix = gather_weights(
        [
            triple_projection_matrix[0],
            selfattend_final_matrix[0],
            sigmoid_expand_matrix[0],
            combine_channel_matrix[0],
        ]
    )
    present_activity = pending_inputs[0]
    made_all = []
    for tick in range(ticks):
        batch_index = sections - 1 - section + tick
        seg_wide = lax.dynamic_index_in_dim(seg_all, batch_index, 0, keepdims=False)
        seg_own = seg_wide[sample_lines : 2 * sample_lines]
        resid = present_activity.astype(jnp.float32)
        normed = layer_norm(resid, selfattend_scaling[0]).astype(jnp.bfloat16)
        projected = jnp.dot(normed, full_qkv, preferred_element_type=jnp.float32)
        query = (projected[:, :feature_count] * (feature_count // HEADS) ** (-0.5)).astype(
            jnp.bfloat16
        )
        keys = projected[:, feature_count : 2 * feature_count].astype(jnp.bfloat16)
        values = projected[:, 2 * feature_count :].astype(jnp.bfloat16)
        wide_keys, wide_values = (
            extended(keys, ((FRAME, 0),), sample_lines),
            extended(values, ((FRAME, 0),), sample_lines),
        )
        context = attend(query, wide_keys, wide_values, seg_wide, seg_own)
        resid = resid + jnp.dot(context, full_out, preferred_element_type=jnp.float32)
        conv_in = layer_norm(resid, depthwise_scaling[0]).astype(jnp.bfloat16)
        doubled = jnp.dot(conv_in, full_glu, preferred_element_type=jnp.float32)
        glu = (doubled[:, :feature_count] * jax.nn.sigmoid(doubled[:, feature_count:])).astype(
            jnp.bfloat16
        )
        wide_glu = extended(glu, ((FRAME, 0),), half)
        depth = depthwise(
            wide_glu,
            seg_wide[sample_lines - half : 2 * sample_lines + half],
            seg_own,
            filter_taps[0],
        )
        act = (depth * jax.nn.sigmoid(depth)).astype(jnp.bfloat16)
        resid = resid + jnp.dot(act, full_mix, preferred_element_type=jnp.float32)
        made = resid.astype(jnp.bfloat16)
        made_all.append(made)
        if tick + 1 < ticks:
            arrived = shifted(made, "section", 1)
            present_activity = jnp.where(section == 0, newcomer_groups[tick], arrived)
    return jnp.stack(made_all)[:, None]


def solution(mesh):
    sections = mesh.shape["section"]
    frames = mesh.shape["frame"]
    mesh = Mesh(mesh.devices.reshape(sections, 2, 4, frames // 8), MESH_AXES)
    in_specs = (
        P(None, FRAME, None),
        P("section", FRAME, None),
        P(None, FRAME),
        P("section", None),
        P("section", FRAME, None),
        P("section", FRAME, None),
        P("section", None),
        P("section", FRAME, None),
        P("section", None, None),
        P("section", FRAME, None),
    )
    out_specs = P(None, "section", FRAME, None)
    return jax.shard_map(
        on_device, mesh=mesh, in_specs=in_specs, out_specs=out_specs, check_vma=False
    )
```

```python
import functools

import jax
import jax.numpy as jnp
from jax import lax
from jax.experimental import pallas as pl
from jax.experimental.pallas import tpu as pltpu
from jax.sharding import Mesh, PartitionSpec as P

HEADS = 24
KERNEL = 31


EPS = 1e-05
FRAME = ("yl", "x", "z")
MESH_AXES = ("section",) + FRAME


def gather_kernel(count, *refs):
    local, gathered = refs[:count], refs[count : 2 * count]
    own_sem, send_sem, recv_sem = refs[2 * count :]
    sizes = {name: lax.axis_size(name) for name in FRAME}
    here = {name: lax.axis_index(name) for name in MESH_AXES}

    def position(coords):
        return (coords["z"] * sizes["x"] + coords["x"]) * sizes["yl"] + coords["yl"]

    def moved(coords, name, step):
        if step == 0:
            return coords
        other = dict(coords)
        other[name] = lax.rem(coords[name] + step + sizes[name], sizes[name])
        return other

    def device(coords):
        return tuple(coords[a] for a in MESH_AXES)

    neighbours = [moved(here, "yl", 1)]
    for name in ("x", "z"):
        neighbours += [moved(here, name, 1), moved(here, name, -1)]
    barrier = pltpu.get_barrier_semaphore()
    for other in neighbours:
        pl.semaphore_signal(
            barrier, inc=1, device_id=device(other), device_id_type=pl.DeviceIdType.MESH
        )
    pl.semaphore_wait(barrier, len(neighbours))

    own_copies = []
    for w in range(count):
        copy = pltpu.make_async_copy(local[w], gathered[w].at[position(here)], own_sem.at[w])
        copy.start()
        own_copies.append(copy)

    counter = [0]

    def send(w, source, target_ref, target):
        index = counter[0]
        counter[0] += 1
        copy = pltpu.make_async_remote_copy(
            src_ref=source,
            dst_ref=target_ref,
            send_sem=send_sem.at[index],
            recv_sem=recv_sem.at[index],
            device_id=device(target),
            device_id_type=pl.DeviceIdType.MESH,
        )
        copy.start()
        return copy

    def run(w, start, blocks, cols):
        return gathered[w].at[pl.ds(position(start), blocks), :, cols]

    def stripe_cols(w, s, part=None):
        width = local[w].shape[-1]
        half = width // 2
        lo, span = (0, half) if s == 0 else (half, width - half)
        if part is None:
            return pl.ds(lo, span)
        quarter = span // 2
        return pl.ds(lo, quarter) if part == 0 else pl.ds(lo + quarter, span - quarter)

    def finish(pending):
        for copy in pending:
            copy.wait()

    base = dict(here)
    base["yl"] = 0
    partner = moved(here, "yl", 1)
    pending = []
    for w in range(count):
        pending.append(send(w, local[w], gathered[w].at[position(here)], partner))
    finish(pending)
    finish(own_copies)
    held = {0: [(base, sizes["yl"])], 1: [(base, sizes["yl"])]}
    orders = {0: ("x", "z"), 1: ("z", "x")}
    for level in range(2):
        pending = []
        for w in range(count):
            for s in (0, 1):
                name = orders[s][level]
                for start, blocks in held[s]:
                    for step in (1, -1):
                        region = run(w, start, blocks, stripe_cols(w, s))
                        pending.append(send(w, region, region, moved(here, name, step)))
        finish(pending)
        pending = []
        for w in range(count):
            for s in (0, 1):
                name = orders[s][level]
                for start, blocks in held[s]:
                    for step, part in ((1, 0), (-1, 1)):
                        region = run(w, moved(start, name, -step), blocks, stripe_cols(w, s, part))
                        pending.append(send(w, region, region, moved(here, name, step)))
        finish(pending)
        for s in (0, 1):
            name = orders[s][level]
            if name == "x" and level == 0:
                start = dict(base)
                start["x"] = 0
                held[s] = [(start, sizes["x"] * sizes["yl"])]
            else:
                held[s] = [
                    (moved(start, name, step), blocks)
                    for start, blocks in held[s]
                    for step in range(sizes[name])
                ]


def copy_count(count):
    return count * (1 + 2 * 2 * (1 + 1) + 2 * 2 * (1 + 4))


def gather_weights(blocks):
    count = len(blocks)
    frames = 1
    for name in FRAME:
        frames *= lax.axis_size(name)
    copies = copy_count(count)
    outs = pl.pallas_call(
        functools.partial(gather_kernel, count),
        out_shape=[jax.ShapeDtypeStruct((frames,) + b.shape, b.dtype) for b in blocks],
        in_specs=[pl.BlockSpec(memory_space=pl.ANY)] * count,
        out_specs=[pl.BlockSpec(memory_space=pl.ANY)] * count,
        scratch_shapes=[
            pltpu.SemaphoreType.DMA((count,)),
            pltpu.SemaphoreType.DMA((copies,)),
            pltpu.SemaphoreType.DMA((copies,)),
        ],
        compiler_params=pltpu.CompilerParams(collective_id=0, has_side_effects=True),
    )(*blocks)
    return [o.reshape(frames * o.shape[1], o.shape[2]) for o in outs]


def gathered_dot(value, weights):
    lines, width = value.shape
    sizes = [lax.axis_size(name) for name in FRAME]
    shaped = value.reshape(lines, *sizes, width // (sizes[0] * sizes[1] * sizes[2]))
    ordered = shaped.transpose(0, 3, 2, 1, 4).reshape(lines, width)
    return jnp.dot(ordered, weights, preferred_element_type=jnp.float32)


def extended(block, sides, width):
    for axis, dim in sides:
        count = lax.axis_size(axis)
        forward = [(i, i + 1) for i in range(count - 1)]
        backward = [(target, source) for source, target in forward]
        low = lax.ppermute(
            lax.slice_in_dim(block, block.shape[dim] - width, None, axis=dim), axis, forward
        )
        high = lax.ppermute(lax.slice_in_dim(block, 0, width, axis=dim), axis, backward)
        block = jnp.concatenate([low, block, high], axis=dim)
    return block


def shifted(value, axis, steps):
    count = lax.axis_size(axis)
    leading, last = (max(0, -steps), min(count, count - steps))
    return lax.ppermute(value, axis, [(source, source + steps) for source in range(leading, last)])


def layer_norm(sample_lines, gain):
    mean = jnp.mean(sample_lines, axis=-1, keepdims=True)
    centred = sample_lines - mean
    spread = jnp.mean(centred * centred, axis=-1, keepdims=True)
    return centred * lax.rsqrt(spread + EPS) * gain


def attend(query, wide_keys, wide_values, seg_wide, seg_own):
    sample_lines, feature_count = query.shape
    head_dim = feature_count // HEADS
    shaped_q = query.reshape(sample_lines, HEADS, head_dim)
    shaped_k = wide_keys.reshape(wide_keys.shape[0], HEADS, head_dim)
    shaped_v = wide_values.reshape(wide_values.shape[0], HEADS, head_dim)
    scores = jnp.einsum("qhd,khd->hqk", shaped_q, shaped_k, preferred_element_type=jnp.float32)
    allowed = (seg_own[:, None] == seg_wide[None, :])[None]
    scores = jnp.where(allowed, scores, -1e30)
    top = jnp.max(scores, axis=-1, keepdims=True)
    expd = jnp.exp(scores - top)
    probs = (expd / jnp.sum(expd, axis=-1, keepdims=True)).astype(jnp.bfloat16)
    context = jnp.einsum("hqk,khd->qhd", probs, shaped_v, preferred_element_type=jnp.float32)
    return context.astype(jnp.bfloat16).reshape(sample_lines, feature_count)


def depthwise(wide_glu, seg_conv, seg_own, taps):
    sample_lines = seg_own.shape[0]
    total = jnp.zeros((sample_lines, wide_glu.shape[1]), jnp.float32)
    for tap in range(taps.shape[0]):
        same = (seg_conv[tap : tap + sample_lines] == seg_own)[:, None]
        total = total + jnp.where(
            same, wide_glu[tap : tap + sample_lines].astype(jnp.float32) * taps[tap], 0.0
        )
    return total


def on_device(
    newcomer_groups,
    pending_inputs,
    speaker_clip_ids,
    selfattend_scaling,
    triple_projection_matrix,
    selfattend_final_matrix,
    depthwise_scaling,
    sigmoid_expand_matrix,
    filter_taps,
    combine_channel_matrix,
):
    sample_lines = pending_inputs.shape[1]
    feature_count = pending_inputs.shape[2]
    half = KERNEL // 2
    sections = lax.axis_size("section")
    section = lax.axis_index("section")
    ticks = newcomer_groups.shape[0] + 1
    seg_all = extended(speaker_clip_ids + 1, ((FRAME, 1),), sample_lines)
    full_qkv, full_out, full_glu, full_mix = gather_weights(
        [
            triple_projection_matrix[0],
            selfattend_final_matrix[0],
            sigmoid_expand_matrix[0],
            combine_channel_matrix[0],
        ]
    )
    present_activity = pending_inputs[0]
    made_all = []
    for tick in range(ticks):
        batch_index = sections - 1 - section + tick
        seg_wide = lax.dynamic_index_in_dim(seg_all, batch_index, 0, keepdims=False)
        seg_own = seg_wide[sample_lines : 2 * sample_lines]
        resid = present_activity.astype(jnp.float32)
        normed = layer_norm(resid, selfattend_scaling[0]).astype(jnp.bfloat16)
        projected = gathered_dot(normed, full_qkv)
        query = (projected[:, :feature_count] * (feature_count // HEADS) ** (-0.5)).astype(
            jnp.bfloat16
        )
        keys = projected[:, feature_count : 2 * feature_count].astype(jnp.bfloat16)
        values = projected[:, 2 * feature_count :].astype(jnp.bfloat16)
        wide_keys, wide_values = (
            extended(keys, ((FRAME, 0),), sample_lines),
            extended(values, ((FRAME, 0),), sample_lines),
        )
        context = attend(query, wide_keys, wide_values, seg_wide, seg_own)
        resid = resid + gathered_dot(context, full_out)
        conv_in = layer_norm(resid, depthwise_scaling[0]).astype(jnp.bfloat16)
        doubled = gathered_dot(conv_in, full_glu)
        glu = (doubled[:, :feature_count] * jax.nn.sigmoid(doubled[:, feature_count:])).astype(
            jnp.bfloat16
        )
        wide_glu = extended(glu, ((FRAME, 0),), half)
        depth = depthwise(
            wide_glu,
            seg_wide[sample_lines - half : 2 * sample_lines + half],
            seg_own,
            filter_taps[0],
        )
        act = (depth * jax.nn.sigmoid(depth)).astype(jnp.bfloat16)
        resid = resid + gathered_dot(act, full_mix)
        made = resid.astype(jnp.bfloat16)
        made_all.append(made)
        if tick + 1 < ticks:
            arrived = shifted(made, "section", 1)
            present_activity = jnp.where(section == 0, newcomer_groups[tick], arrived)
    return jnp.stack(made_all)[:, None]


def solution(mesh):
    sections = mesh.shape["section"]
    frames = mesh.shape["frame"]
    mesh = Mesh(mesh.devices.reshape(sections, 2, 4, frames // 8), MESH_AXES)
    in_specs = (
        P(None, FRAME, None),
        P("section", FRAME, None),
        P(None, FRAME),
        P("section", None),
        P("section", FRAME, None),
        P("section", FRAME, None),
        P("section", None),
        P("section", FRAME, None),
        P("section", None, None),
        P("section", FRAME, None),
    )
    out_specs = P(None, "section", FRAME, None)
    return jax.shard_map(
        on_device, mesh=mesh, in_specs=in_specs, out_specs=out_specs, check_vma=False
    )
```

```python
import functools

import jax
import jax.numpy as jnp
from jax import lax
from jax.experimental import pallas as pl
from jax.experimental.pallas import tpu as pltpu
from jax.sharding import Mesh, PartitionSpec as P

HEADS = 24
KERNEL = 31


EPS = 1e-05
FRAME = ("yl", "x", "z")
MESH_AXES = ("section",) + FRAME


def gather_kernel(count, *refs):
    local, gathered = refs[:count], refs[count : 2 * count]
    own_sem, send_sem, recv_sem = refs[2 * count :]
    sizes = {name: lax.axis_size(name) for name in FRAME}
    here = {name: lax.axis_index(name) for name in MESH_AXES}

    def position(coords):
        return (coords["yl"] * sizes["x"] + coords["x"]) * sizes["z"] + coords["z"]

    def moved(coords, name, step):
        if step == 0:
            return coords
        other = dict(coords)
        other[name] = lax.rem(coords[name] + step + sizes[name], sizes[name])
        return other

    neighbours = [moved(here, "yl", 1)]
    for name in ("x", "z"):
        neighbours += [moved(here, name, 1), moved(here, name, -1)]
    barrier = pltpu.get_barrier_semaphore()
    for other in neighbours:
        pl.semaphore_signal(
            barrier, inc=1, device_id=tuple(other[a] for a in MESH_AXES),
            device_id_type=pl.DeviceIdType.MESH,
        )
    pl.semaphore_wait(barrier, len(neighbours))

    own_copies = []
    for w in range(count):
        copy = pltpu.make_async_copy(local[w], gathered[w].at[position(here)], own_sem.at[w])
        copy.start()
        own_copies.append(copy)

    counter = [0]

    def send(w, coords, cols, target):
        index = counter[0]
        counter[0] += 1
        if coords is here:
            source = local[w].at[:, cols]
        else:
            source = gathered[w].at[position(coords), :, cols]
        copy = pltpu.make_async_remote_copy(
            src_ref=source,
            dst_ref=gathered[w].at[position(coords), :, cols],
            send_sem=send_sem.at[index],
            recv_sem=recv_sem.at[index],
            device_id=tuple(target[a] for a in MESH_AXES),
            device_id_type=pl.DeviceIdType.MESH,
        )
        copy.start()
        return copy

    widths = [r.shape[-1] for r in local]
    orders = (("x", "z"), ("z", "x"))
    held = [[[here] for _ in orders] for _ in range(count)]

    def stripe_cols(w, s, part=None):
        half = widths[w] // 2
        lo, width = (0, half) if s == 0 else (half, widths[w] - half)
        if part is None:
            return pl.ds(lo, width)
        quarter = width // 2
        return pl.ds(lo, quarter) if part == 0 else pl.ds(lo + quarter, width - quarter)

    partner = moved(here, "yl", 1)
    pending = []
    for w in range(count):
        for s, order in enumerate(orders):
            pending.append(send(w, here, stripe_cols(w, s), partner))
            for step in (1, -1):
                pending.append(send(w, here, stripe_cols(w, s), moved(here, order[0], step)))
    for copy in pending:
        copy.wait()
    for origin in (None, partner):
        pending = []
        for w in range(count):
            for s, order in enumerate(orders):
                name = order[0]
                if origin is None:
                    for step in (1, -1):
                        pending.append(send(w, partner, stripe_cols(w, s), moved(here, name, step)))
                    source = here
                else:
                    source = partner
                pending.append(
                    send(w, moved(source, name, -1), stripe_cols(w, s, 0), moved(here, name, 1))
                )
                pending.append(
                    send(w, moved(source, name, 1), stripe_cols(w, s, 1), moved(here, name, -1))
                )
        for copy in pending:
            copy.wait()
    for w in range(count):
        for s, order in enumerate(orders):
            held[w][s] = [moved(c, order[0], step) for c in (here, partner) for step in (0, 1, 2, 3)]
    for level in range(1, 2):
        pending = []
        for w in range(count):
            for s, order in enumerate(orders):
                name = order[level]
                for coords in held[w][s]:
                    for step in (1, -1):
                        pending.append(send(w, coords, stripe_cols(w, s), moved(here, name, step)))
        for copy in pending:
            copy.wait()
        pending = []
        for w in range(count):
            for s, order in enumerate(orders):
                name = order[level]
                for coords in held[w][s]:
                    pending.append(
                        send(w, moved(coords, name, -1), stripe_cols(w, s, 0), moved(here, name, 1))
                    )
                    pending.append(
                        send(w, moved(coords, name, 1), stripe_cols(w, s, 1), moved(here, name, -1))
                    )
        for copy in pending:
            copy.wait()
        for w in range(count):
            for s, order in enumerate(orders):
                name = order[level]
                held[w][s] = [moved(c, name, step) for c in held[w][s] for step in (0, 1, 2, 3)]
    for copy in own_copies:
        copy.wait()


def gather_weights(blocks):
    count = len(blocks)
    frames = 1
    for name in FRAME:
        frames *= lax.axis_size(name)
    copies = count * 2 * (1 + 2 * (4 + 4 * 4))
    outs = pl.pallas_call(
        functools.partial(gather_kernel, count),
        out_shape=[jax.ShapeDtypeStruct((frames,) + b.shape, b.dtype) for b in blocks],
        in_specs=[pl.BlockSpec(memory_space=pl.ANY)] * count,
        out_specs=[pl.BlockSpec(memory_space=pl.ANY)] * count,
        scratch_shapes=[
            pltpu.SemaphoreType.DMA((count,)),
            pltpu.SemaphoreType.DMA((copies,)),
            pltpu.SemaphoreType.DMA((copies,)),
        ],
        compiler_params=pltpu.CompilerParams(collective_id=0, has_side_effects=True),
    )(*blocks)
    return [o.reshape(frames * o.shape[1], o.shape[2]) for o in outs]


def extended(block, sides, width):
    for axis, dim in sides:
        count = lax.axis_size(axis)
        forward = [(i, i + 1) for i in range(count - 1)]
        backward = [(target, source) for source, target in forward]
        low = lax.ppermute(
            lax.slice_in_dim(block, block.shape[dim] - width, None, axis=dim), axis, forward
        )
        high = lax.ppermute(lax.slice_in_dim(block, 0, width, axis=dim), axis, backward)
        block = jnp.concatenate([low, block, high], axis=dim)
    return block


def shifted(value, axis, steps):
    count = lax.axis_size(axis)
    leading, last = (max(0, -steps), min(count, count - steps))
    return lax.ppermute(value, axis, [(source, source + steps) for source in range(leading, last)])


def layer_norm(sample_lines, gain):
    mean = jnp.mean(sample_lines, axis=-1, keepdims=True)
    centred = sample_lines - mean
    spread = jnp.mean(centred * centred, axis=-1, keepdims=True)
    return centred * lax.rsqrt(spread + EPS) * gain


def attend(query, wide_keys, wide_values, seg_wide, seg_own):
    sample_lines, feature_count = query.shape
    head_dim = feature_count // HEADS
    shaped_q = query.reshape(sample_lines, HEADS, head_dim)
    shaped_k = wide_keys.reshape(wide_keys.shape[0], HEADS, head_dim)
    shaped_v = wide_values.reshape(wide_values.shape[0], HEADS, head_dim)
    scores = jnp.einsum("qhd,khd->hqk", shaped_q, shaped_k, preferred_element_type=jnp.float32)
    allowed = (seg_own[:, None] == seg_wide[None, :])[None]
    scores = jnp.where(allowed, scores, -1e30)
    top = jnp.max(scores, axis=-1, keepdims=True)
    expd = jnp.exp(scores - top)
    probs = (expd / jnp.sum(expd, axis=-1, keepdims=True)).astype(jnp.bfloat16)
    context = jnp.einsum("hqk,khd->qhd", probs, shaped_v, preferred_element_type=jnp.float32)
    return context.astype(jnp.bfloat16).reshape(sample_lines, feature_count)


def depthwise(wide_glu, seg_conv, seg_own, taps):
    sample_lines = seg_own.shape[0]
    total = jnp.zeros((sample_lines, wide_glu.shape[1]), jnp.float32)
    for tap in range(taps.shape[0]):
        same = (seg_conv[tap : tap + sample_lines] == seg_own)[:, None]
        total = total + jnp.where(
            same, wide_glu[tap : tap + sample_lines].astype(jnp.float32) * taps[tap], 0.0
        )
    return total


def on_device(
    newcomer_groups,
    pending_inputs,
    speaker_clip_ids,
    selfattend_scaling,
    triple_projection_matrix,
    selfattend_final_matrix,
    depthwise_scaling,
    sigmoid_expand_matrix,
    filter_taps,
    combine_channel_matrix,
):
    sample_lines = pending_inputs.shape[1]
    feature_count = pending_inputs.shape[2]
    half = KERNEL // 2
    sections = lax.axis_size("section")
    section = lax.axis_index("section")
    ticks = newcomer_groups.shape[0] + 1
    seg_all = extended(speaker_clip_ids + 1, ((FRAME, 1),), sample_lines)
    full_qkv, full_out, full_glu, full_mix = gather_weights(
        [
            triple_projection_matrix[0],
            selfattend_final_matrix[0],
            sigmoid_expand_matrix[0],
            combine_channel_matrix[0],
        ]
    )
    present_activity = pending_inputs[0]
    made_all = []
    for tick in range(ticks):
        batch_index = sections - 1 - section + tick
        seg_wide = lax.dynamic_index_in_dim(seg_all, batch_index, 0, keepdims=False)
        seg_own = seg_wide[sample_lines : 2 * sample_lines]
        resid = present_activity.astype(jnp.float32)
        normed = layer_norm(resid, selfattend_scaling[0]).astype(jnp.bfloat16)
        projected = jnp.dot(normed, full_qkv, preferred_element_type=jnp.float32)
        query = (projected[:, :feature_count] * (feature_count // HEADS) ** (-0.5)).astype(
            jnp.bfloat16
        )
        keys = projected[:, feature_count : 2 * feature_count].astype(jnp.bfloat16)
        values = projected[:, 2 * feature_count :].astype(jnp.bfloat16)
        wide_keys, wide_values = (
            extended(keys, ((FRAME, 0),), sample_lines),
            extended(values, ((FRAME, 0),), sample_lines),
        )
        context = attend(query, wide_keys, wide_values, seg_wide, seg_own)
        resid = resid + jnp.dot(context, full_out, preferred_element_type=jnp.float32)
        conv_in = layer_norm(resid, depthwise_scaling[0]).astype(jnp.bfloat16)
        doubled = jnp.dot(conv_in, full_glu, preferred_element_type=jnp.float32)
        glu = (doubled[:, :feature_count] * jax.nn.sigmoid(doubled[:, feature_count:])).astype(
            jnp.bfloat16
        )
        wide_glu = extended(glu, ((FRAME, 0),), half)
        depth = depthwise(
            wide_glu,
            seg_wide[sample_lines - half : 2 * sample_lines + half],
            seg_own,
            filter_taps[0],
        )
        act = (depth * jax.nn.sigmoid(depth)).astype(jnp.bfloat16)
        resid = resid + jnp.dot(act, full_mix, preferred_element_type=jnp.float32)
        made = resid.astype(jnp.bfloat16)
        made_all.append(made)
        if tick + 1 < ticks:
            arrived = shifted(made, "section", 1)
            present_activity = jnp.where(section == 0, newcomer_groups[tick], arrived)
    return jnp.stack(made_all)[:, None]


def solution(mesh):
    sections = mesh.shape["section"]
    frames = mesh.shape["frame"]
    mesh = Mesh(mesh.devices.reshape(sections, 2, 4, frames // 8), MESH_AXES)
    in_specs = (
        P(None, FRAME, None),
        P("section", FRAME, None),
        P(None, FRAME),
        P("section", None),
        P("section", FRAME, None),
        P("section", FRAME, None),
        P("section", None),
        P("section", FRAME, None),
        P("section", None, None),
        P("section", FRAME, None),
    )
    out_specs = P(None, "section", FRAME, None)
    return jax.shard_map(
        on_device, mesh=mesh, in_specs=in_specs, out_specs=out_specs, check_vma=False
    )
```

```python
import functools

import jax
import jax.numpy as jnp
from jax import lax
from jax.experimental import pallas as pl
from jax.experimental.pallas import tpu as pltpu
from jax.sharding import Mesh, PartitionSpec as P

HEADS = 24
KERNEL = 31


EPS = 1e-05
FRAME = ("yl", "x", "z")
MESH_AXES = ("section",) + FRAME


def gather_kernel(count, *refs):
    local, gathered = refs[:count], refs[count : 2 * count]
    own_sem, send_sem, recv_sem = refs[2 * count :]
    sizes = {name: lax.axis_size(name) for name in FRAME}
    here = {name: lax.axis_index(name) for name in MESH_AXES}

    def position(coords):
        return (coords["yl"] * sizes["x"] + coords["x"]) * sizes["z"] + coords["z"]

    def moved(coords, name, step):
        if step == 0:
            return coords
        other = dict(coords)
        other[name] = lax.rem(coords[name] + step + sizes[name], sizes[name])
        return other

    neighbours = [moved(here, "yl", 1)]
    for name in ("x", "z"):
        neighbours += [moved(here, name, 1), moved(here, name, -1)]
    barrier = pltpu.get_barrier_semaphore()
    for other in neighbours:
        pl.semaphore_signal(
            barrier, inc=1, device_id=tuple(other[a] for a in MESH_AXES),
            device_id_type=pl.DeviceIdType.MESH,
        )
    pl.semaphore_wait(barrier, len(neighbours))

    own_copies = []
    for w in range(count):
        copy = pltpu.make_async_copy(local[w], gathered[w].at[position(here)], own_sem.at[w])
        copy.start()
        own_copies.append(copy)

    counter = [0]

    def send(w, coords, cols, target):
        index = counter[0]
        counter[0] += 1
        if coords is here:
            source = local[w].at[:, cols]
        else:
            source = gathered[w].at[position(coords), :, cols]
        copy = pltpu.make_async_remote_copy(
            src_ref=source,
            dst_ref=gathered[w].at[position(coords), :, cols],
            send_sem=send_sem.at[index],
            recv_sem=recv_sem.at[index],
            device_id=tuple(target[a] for a in MESH_AXES),
            device_id_type=pl.DeviceIdType.MESH,
        )
        copy.start()
        return copy

    widths = [r.shape[-1] for r in local]
    orders = (("x", "z"), ("z", "x"))
    held = [[[here] for _ in orders] for _ in range(count)]

    def stripe_cols(w, s, part=None):
        half = widths[w] // 2
        lo, width = (0, half) if s == 0 else (half, widths[w] - half)
        if part is None:
            return pl.ds(lo, width)
        quarter = width // 2
        return pl.ds(lo, quarter) if part == 0 else pl.ds(lo + quarter, width - quarter)

    partner = moved(here, "yl", 1)
    pending = []
    for w in range(count):
        for s, order in enumerate(orders):
            pending.append(send(w, here, stripe_cols(w, s), partner))
            for name in order:
                for step in (1, -1):
                    pending.append(send(w, here, stripe_cols(w, s), moved(here, name, step)))
    for copy in pending:
        copy.wait()
    for origin in (None, partner):
        pending = []
        for w in range(count):
            for s, order in enumerate(orders):
                name = order[0]
                if origin is None:
                    for step in (1, -1):
                        pending.append(send(w, partner, stripe_cols(w, s), moved(here, name, step)))
                    source = here
                else:
                    source = partner
                pending.append(
                    send(w, moved(source, name, -1), stripe_cols(w, s, 0), moved(here, name, 1))
                )
                pending.append(
                    send(w, moved(source, name, 1), stripe_cols(w, s, 1), moved(here, name, -1))
                )
        for copy in pending:
            copy.wait()
    for w in range(count):
        for s, order in enumerate(orders):
            held[w][s] = [moved(c, order[0], step) for c in (here, partner) for step in (0, 1, 2, 3)]
    for level in range(1, 2):
        pending = []
        for w in range(count):
            for s, order in enumerate(orders):
                name = order[level]
                for coords in held[w][s]:
                    if coords is here:
                        continue
                    for step in (1, -1):
                        pending.append(send(w, coords, stripe_cols(w, s), moved(here, name, step)))
        for copy in pending:
            copy.wait()
        pending = []
        for w in range(count):
            for s, order in enumerate(orders):
                name = order[level]
                for coords in held[w][s]:
                    pending.append(
                        send(w, moved(coords, name, -1), stripe_cols(w, s, 0), moved(here, name, 1))
                    )
                    pending.append(
                        send(w, moved(coords, name, 1), stripe_cols(w, s, 1), moved(here, name, -1))
                    )
        for copy in pending:
            copy.wait()
        for w in range(count):
            for s, order in enumerate(orders):
                name = order[level]
                held[w][s] = [moved(c, name, step) for c in held[w][s] for step in (0, 1, 2, 3)]
    for copy in own_copies:
        copy.wait()


def gather_weights(blocks):
    count = len(blocks)
    frames = 1
    for name in FRAME:
        frames *= lax.axis_size(name)
    copies = count * 2 * (1 + 2 * (4 + 4 * 4))
    outs = pl.pallas_call(
        functools.partial(gather_kernel, count),
        out_shape=[jax.ShapeDtypeStruct((frames,) + b.shape, b.dtype) for b in blocks],
        in_specs=[pl.BlockSpec(memory_space=pl.ANY)] * count,
        out_specs=[pl.BlockSpec(memory_space=pl.ANY)] * count,
        scratch_shapes=[
            pltpu.SemaphoreType.DMA((count,)),
            pltpu.SemaphoreType.DMA((copies,)),
            pltpu.SemaphoreType.DMA((copies,)),
        ],
        compiler_params=pltpu.CompilerParams(collective_id=0, has_side_effects=True),
    )(*blocks)
    return [o.reshape(frames * o.shape[1], o.shape[2]) for o in outs]


def extended(block, sides, width):
    for axis, dim in sides:
        count = lax.axis_size(axis)
        forward = [(i, i + 1) for i in range(count - 1)]
        backward = [(target, source) for source, target in forward]
        low = lax.ppermute(
            lax.slice_in_dim(block, block.shape[dim] - width, None, axis=dim), axis, forward
        )
        high = lax.ppermute(lax.slice_in_dim(block, 0, width, axis=dim), axis, backward)
        block = jnp.concatenate([low, block, high], axis=dim)
    return block


def shifted(value, axis, steps):
    count = lax.axis_size(axis)
    leading, last = (max(0, -steps), min(count, count - steps))
    return lax.ppermute(value, axis, [(source, source + steps) for source in range(leading, last)])


def layer_norm(sample_lines, gain):
    mean = jnp.mean(sample_lines, axis=-1, keepdims=True)
    centred = sample_lines - mean
    spread = jnp.mean(centred * centred, axis=-1, keepdims=True)
    return centred * lax.rsqrt(spread + EPS) * gain


def attend(query, wide_keys, wide_values, seg_wide, seg_own):
    sample_lines, feature_count = query.shape
    head_dim = feature_count // HEADS
    shaped_q = query.reshape(sample_lines, HEADS, head_dim)
    shaped_k = wide_keys.reshape(wide_keys.shape[0], HEADS, head_dim)
    shaped_v = wide_values.reshape(wide_values.shape[0], HEADS, head_dim)
    scores = jnp.einsum("qhd,khd->hqk", shaped_q, shaped_k, preferred_element_type=jnp.float32)
    allowed = (seg_own[:, None] == seg_wide[None, :])[None]
    scores = jnp.where(allowed, scores, -1e30)
    top = jnp.max(scores, axis=-1, keepdims=True)
    expd = jnp.exp(scores - top)
    probs = (expd / jnp.sum(expd, axis=-1, keepdims=True)).astype(jnp.bfloat16)
    context = jnp.einsum("hqk,khd->qhd", probs, shaped_v, preferred_element_type=jnp.float32)
    return context.astype(jnp.bfloat16).reshape(sample_lines, feature_count)


def depthwise(wide_glu, seg_conv, seg_own, taps):
    sample_lines = seg_own.shape[0]
    total = jnp.zeros((sample_lines, wide_glu.shape[1]), jnp.float32)
    for tap in range(taps.shape[0]):
        same = (seg_conv[tap : tap + sample_lines] == seg_own)[:, None]
        total = total + jnp.where(
            same, wide_glu[tap : tap + sample_lines].astype(jnp.float32) * taps[tap], 0.0
        )
    return total


def on_device(
    newcomer_groups,
    pending_inputs,
    speaker_clip_ids,
    selfattend_scaling,
    triple_projection_matrix,
    selfattend_final_matrix,
    depthwise_scaling,
    sigmoid_expand_matrix,
    filter_taps,
    combine_channel_matrix,
):
    sample_lines = pending_inputs.shape[1]
    feature_count = pending_inputs.shape[2]
    half = KERNEL // 2
    sections = lax.axis_size("section")
    section = lax.axis_index("section")
    ticks = newcomer_groups.shape[0] + 1
    seg_all = extended(speaker_clip_ids + 1, ((FRAME, 1),), sample_lines)
    full_qkv, full_out, full_glu, full_mix = gather_weights(
        [
            triple_projection_matrix[0],
            selfattend_final_matrix[0],
            sigmoid_expand_matrix[0],
            combine_channel_matrix[0],
        ]
    )
    present_activity = pending_inputs[0]
    made_all = []
    for tick in range(ticks):
        batch_index = sections - 1 - section + tick
        seg_wide = lax.dynamic_index_in_dim(seg_all, batch_index, 0, keepdims=False)
        seg_own = seg_wide[sample_lines : 2 * sample_lines]
        resid = present_activity.astype(jnp.float32)
        normed = layer_norm(resid, selfattend_scaling[0]).astype(jnp.bfloat16)
        projected = jnp.dot(normed, full_qkv, preferred_element_type=jnp.float32)
        query = (projected[:, :feature_count] * (feature_count // HEADS) ** (-0.5)).astype(
            jnp.bfloat16
        )
        keys = projected[:, feature_count : 2 * feature_count].astype(jnp.bfloat16)
        values = projected[:, 2 * feature_count :].astype(jnp.bfloat16)
        wide_keys, wide_values = (
            extended(keys, ((FRAME, 0),), sample_lines),
            extended(values, ((FRAME, 0),), sample_lines),
        )
        context = attend(query, wide_keys, wide_values, seg_wide, seg_own)
        resid = resid + jnp.dot(context, full_out, preferred_element_type=jnp.float32)
        conv_in = layer_norm(resid, depthwise_scaling[0]).astype(jnp.bfloat16)
        doubled = jnp.dot(conv_in, full_glu, preferred_element_type=jnp.float32)
        glu = (doubled[:, :feature_count] * jax.nn.sigmoid(doubled[:, feature_count:])).astype(
            jnp.bfloat16
        )
        wide_glu = extended(glu, ((FRAME, 0),), half)
        depth = depthwise(
            wide_glu,
            seg_wide[sample_lines - half : 2 * sample_lines + half],
            seg_own,
            filter_taps[0],
        )
        act = (depth * jax.nn.sigmoid(depth)).astype(jnp.bfloat16)
        resid = resid + jnp.dot(act, full_mix, preferred_element_type=jnp.float32)
        made = resid.astype(jnp.bfloat16)
        made_all.append(made)
        if tick + 1 < ticks:
            arrived = shifted(made, "section", 1)
            present_activity = jnp.where(section == 0, newcomer_groups[tick], arrived)
    return jnp.stack(made_all)[:, None]


def solution(mesh):
    sections = mesh.shape["section"]
    frames = mesh.shape["frame"]
    mesh = Mesh(mesh.devices.reshape(sections, 2, 4, frames // 8), MESH_AXES)
    in_specs = (
        P(None, FRAME, None),
        P("section", FRAME, None),
        P(None, FRAME),
        P("section", None),
        P("section", FRAME, None),
        P("section", FRAME, None),
        P("section", None),
        P("section", FRAME, None),
        P("section", None, None),
        P("section", FRAME, None),
    )
    out_specs = P(None, "section", FRAME, None)
    return jax.shard_map(
        on_device, mesh=mesh, in_specs=in_specs, out_specs=out_specs, check_vma=False
    )
```

```python
import functools

import jax
import jax.numpy as jnp
from jax import lax
from jax.experimental import pallas as pl
from jax.experimental.pallas import tpu as pltpu
from jax.sharding import Mesh, PartitionSpec as P

HEADS = 24
KERNEL = 31


EPS = 1e-05
FRAME = ("yl", "x", "z")
MESH_AXES = ("section",) + FRAME


def gather_kernel(count, *refs):
    local, gathered = refs[:count], refs[count : 2 * count]
    own_sem, send_sem, recv_sem = refs[2 * count :]
    sizes = {name: lax.axis_size(name) for name in FRAME}
    here = {name: lax.axis_index(name) for name in MESH_AXES}

    def position(coords):
        return (coords["yl"] * sizes["x"] + coords["x"]) * sizes["z"] + coords["z"]

    def moved(coords, name, step):
        if step == 0:
            return coords
        other = dict(coords)
        other[name] = lax.rem(coords[name] + step + sizes[name], sizes[name])
        return other

    neighbours = [moved(here, "yl", 1)]
    for name in ("x", "z"):
        neighbours += [moved(here, name, 1), moved(here, name, -1)]
    barrier = pltpu.get_barrier_semaphore()
    for other in neighbours:
        pl.semaphore_signal(
            barrier, inc=1, device_id=tuple(other[a] for a in MESH_AXES),
            device_id_type=pl.DeviceIdType.MESH,
        )
    pl.semaphore_wait(barrier, len(neighbours))

    own_copies = []
    for w in range(count):
        copy = pltpu.make_async_copy(local[w], gathered[w].at[position(here)], own_sem.at[w])
        copy.start()
        own_copies.append(copy)

    counter = [0]

    def send(w, coords, cols, target):
        index = counter[0]
        counter[0] += 1
        if coords is here:
            source = local[w].at[:, cols]
        else:
            source = gathered[w].at[position(coords), :, cols]
        copy = pltpu.make_async_remote_copy(
            src_ref=source,
            dst_ref=gathered[w].at[position(coords), :, cols],
            send_sem=send_sem.at[index],
            recv_sem=recv_sem.at[index],
            device_id=tuple(target[a] for a in MESH_AXES),
            device_id_type=pl.DeviceIdType.MESH,
        )
        copy.start()
        return copy

    widths = [r.shape[-1] for r in local]
    orders = (("x", "z"), ("z", "x"))
    held = [[[here] for _ in orders] for _ in range(count)]

    def stripe_cols(w, s, part=None):
        half = widths[w] // 2
        lo, width = (0, half) if s == 0 else (half, widths[w] - half)
        if part is None:
            return pl.ds(lo, width)
        quarter = width // 2
        return pl.ds(lo, quarter) if part == 0 else pl.ds(lo + quarter, width - quarter)

    partner = moved(here, "yl", 1)
    pending = []
    for w in range(count):
        for s, order in enumerate(orders):
            pending.append(send(w, here, stripe_cols(w, s), partner))
            for name in order:
                for step in (1, -1):
                    pending.append(send(w, here, stripe_cols(w, s), moved(here, name, step)))
    for copy in pending:
        copy.wait()
    for origin in (None, partner):
        pending = []
        for w in range(count):
            for s, order in enumerate(orders):
                name = order[0]
                if origin is None:
                    for step in (1, -1):
                        pending.append(send(w, partner, stripe_cols(w, s), moved(here, name, step)))
                    source = here
                else:
                    source = partner
                pending.append(
                    send(w, moved(source, name, -1), stripe_cols(w, s, 0), moved(here, name, 1))
                )
                pending.append(
                    send(w, moved(source, name, 1), stripe_cols(w, s, 1), moved(here, name, -1))
                )
        for copy in pending:
            copy.wait()
    for w in range(count):
        for s, order in enumerate(orders):
            held[w][s] = [moved(c, order[0], step) for c in (here, partner) for step in (0, 1, 2, 3)]
    level = 1
    forwards = []

    def forward(w, s, name, coords, step):
        part = 0 if step == 1 else 1
        forwards.append(
            send(w, moved(coords, name, -step), stripe_cols(w, s, part), moved(here, name, step))
        )

    for w in range(count):
        for s, order in enumerate(orders):
            for step in (1, -1):
                forward(w, s, order[level], here, step)
    pending = []
    for w in range(count):
        for s, order in enumerate(orders):
            name = order[level]
            for coords in held[w][s]:
                if coords is here:
                    continue
                for step in (1, -1):
                    copy = send(w, coords, stripe_cols(w, s), moved(here, name, step))
                    pending.append((copy, w, s, name, coords, step))
    for copy, w, s, name, coords, step in pending:
        copy.wait()
        forward(w, s, name, coords, step)
    for copy in forwards:
        copy.wait()
    for copy in own_copies:
        copy.wait()


def gather_weights(blocks):
    count = len(blocks)
    frames = 1
    for name in FRAME:
        frames *= lax.axis_size(name)
    copies = count * 2 * (1 + 2 * (4 + 4 * 4))
    outs = pl.pallas_call(
        functools.partial(gather_kernel, count),
        out_shape=[jax.ShapeDtypeStruct((frames,) + b.shape, b.dtype) for b in blocks],
        in_specs=[pl.BlockSpec(memory_space=pl.ANY)] * count,
        out_specs=[pl.BlockSpec(memory_space=pl.ANY)] * count,
        scratch_shapes=[
            pltpu.SemaphoreType.DMA((count,)),
            pltpu.SemaphoreType.DMA((copies,)),
            pltpu.SemaphoreType.DMA((copies,)),
        ],
        compiler_params=pltpu.CompilerParams(collective_id=0, has_side_effects=True),
    )(*blocks)
    return [o.reshape(frames * o.shape[1], o.shape[2]) for o in outs]


def extended(block, sides, width):
    for axis, dim in sides:
        count = lax.axis_size(axis)
        forward = [(i, i + 1) for i in range(count - 1)]
        backward = [(target, source) for source, target in forward]
        low = lax.ppermute(
            lax.slice_in_dim(block, block.shape[dim] - width, None, axis=dim), axis, forward
        )
        high = lax.ppermute(lax.slice_in_dim(block, 0, width, axis=dim), axis, backward)
        block = jnp.concatenate([low, block, high], axis=dim)
    return block


def shifted(value, axis, steps):
    count = lax.axis_size(axis)
    leading, last = (max(0, -steps), min(count, count - steps))
    return lax.ppermute(value, axis, [(source, source + steps) for source in range(leading, last)])


def layer_norm(sample_lines, gain):
    mean = jnp.mean(sample_lines, axis=-1, keepdims=True)
    centred = sample_lines - mean
    spread = jnp.mean(centred * centred, axis=-1, keepdims=True)
    return centred * lax.rsqrt(spread + EPS) * gain


def attend(query, wide_keys, wide_values, seg_wide, seg_own):
    sample_lines, feature_count = query.shape
    head_dim = feature_count // HEADS
    shaped_q = query.reshape(sample_lines, HEADS, head_dim)
    shaped_k = wide_keys.reshape(wide_keys.shape[0], HEADS, head_dim)
    shaped_v = wide_values.reshape(wide_values.shape[0], HEADS, head_dim)
    scores = jnp.einsum("qhd,khd->hqk", shaped_q, shaped_k, preferred_element_type=jnp.float32)
    allowed = (seg_own[:, None] == seg_wide[None, :])[None]
    scores = jnp.where(allowed, scores, -1e30)
    top = jnp.max(scores, axis=-1, keepdims=True)
    expd = jnp.exp(scores - top)
    probs = (expd / jnp.sum(expd, axis=-1, keepdims=True)).astype(jnp.bfloat16)
    context = jnp.einsum("hqk,khd->qhd", probs, shaped_v, preferred_element_type=jnp.float32)
    return context.astype(jnp.bfloat16).reshape(sample_lines, feature_count)


def depthwise(wide_glu, seg_conv, seg_own, taps):
    sample_lines = seg_own.shape[0]
    total = jnp.zeros((sample_lines, wide_glu.shape[1]), jnp.float32)
    for tap in range(taps.shape[0]):
        same = (seg_conv[tap : tap + sample_lines] == seg_own)[:, None]
        total = total + jnp.where(
            same, wide_glu[tap : tap + sample_lines].astype(jnp.float32) * taps[tap], 0.0
        )
    return total


def on_device(
    newcomer_groups,
    pending_inputs,
    speaker_clip_ids,
    selfattend_scaling,
    triple_projection_matrix,
    selfattend_final_matrix,
    depthwise_scaling,
    sigmoid_expand_matrix,
    filter_taps,
    combine_channel_matrix,
):
    sample_lines = pending_inputs.shape[1]
    feature_count = pending_inputs.shape[2]
    half = KERNEL // 2
    sections = lax.axis_size("section")
    section = lax.axis_index("section")
    ticks = newcomer_groups.shape[0] + 1
    seg_all = extended(speaker_clip_ids + 1, ((FRAME, 1),), sample_lines)
    full_qkv, full_out, full_glu, full_mix = gather_weights(
        [
            triple_projection_matrix[0],
            selfattend_final_matrix[0],
            sigmoid_expand_matrix[0],
            combine_channel_matrix[0],
        ]
    )
    present_activity = pending_inputs[0]
    made_all = []
    for tick in range(ticks):
        batch_index = sections - 1 - section + tick
        seg_wide = lax.dynamic_index_in_dim(seg_all, batch_index, 0, keepdims=False)
        seg_own = seg_wide[sample_lines : 2 * sample_lines]
        resid = present_activity.astype(jnp.float32)
        normed = layer_norm(resid, selfattend_scaling[0]).astype(jnp.bfloat16)
        projected = jnp.dot(normed, full_qkv, preferred_element_type=jnp.float32)
        query = (projected[:, :feature_count] * (feature_count // HEADS) ** (-0.5)).astype(
            jnp.bfloat16
        )
        keys = projected[:, feature_count : 2 * feature_count].astype(jnp.bfloat16)
        values = projected[:, 2 * feature_count :].astype(jnp.bfloat16)
        wide_keys, wide_values = (
            extended(keys, ((FRAME, 0),), sample_lines),
            extended(values, ((FRAME, 0),), sample_lines),
        )
        context = attend(query, wide_keys, wide_values, seg_wide, seg_own)
        resid = resid + jnp.dot(context, full_out, preferred_element_type=jnp.float32)
        conv_in = layer_norm(resid, depthwise_scaling[0]).astype(jnp.bfloat16)
        doubled = jnp.dot(conv_in, full_glu, preferred_element_type=jnp.float32)
        glu = (doubled[:, :feature_count] * jax.nn.sigmoid(doubled[:, feature_count:])).astype(
            jnp.bfloat16
        )
        wide_glu = extended(glu, ((FRAME, 0),), half)
        depth = depthwise(
            wide_glu,
            seg_wide[sample_lines - half : 2 * sample_lines + half],
            seg_own,
            filter_taps[0],
        )
        act = (depth * jax.nn.sigmoid(depth)).astype(jnp.bfloat16)
        resid = resid + jnp.dot(act, full_mix, preferred_element_type=jnp.float32)
        made = resid.astype(jnp.bfloat16)
        made_all.append(made)
        if tick + 1 < ticks:
            arrived = shifted(made, "section", 1)
            present_activity = jnp.where(section == 0, newcomer_groups[tick], arrived)
    return jnp.stack(made_all)[:, None]


def solution(mesh):
    sections = mesh.shape["section"]
    frames = mesh.shape["frame"]
    mesh = Mesh(mesh.devices.reshape(sections, 2, 4, frames // 8), MESH_AXES)
    in_specs = (
        P(None, FRAME, None),
        P("section", FRAME, None),
        P(None, FRAME),
        P("section", None),
        P("section", FRAME, None),
        P("section", FRAME, None),
        P("section", None),
        P("section", FRAME, None),
        P("section", None, None),
        P("section", FRAME, None),
    )
    out_specs = P(None, "section", FRAME, None)
    return jax.shard_map(
        on_device, mesh=mesh, in_specs=in_specs, out_specs=out_specs, check_vma=False
    )
```
